512 devices in a mesh: lat: 64 (over z_lo, y, core), rad: 8 (over x, z_hi).
Axes of the slice: x: 4, y: 8, z: 8 (z_hi: 2, z_lo: 4; z = z_hi * 4 + z_lo), core: 2. Of those that a mesh axis runs over, the one named last changes fastest.
Arguments:
- displacement: float32 [1024, 32, 2048], P('lat', 'rad'), may hold values from -3 to 3
- memory: float32 [1024, 32, 2048], P('lat', 'rad'), may hold values from -3 to 3
- ice_class: int32 [1024, 2048], P('lat'), may hold values from 0 to 7
- material: int32 [1024, 32], P('lat', 'rad'), may hold values from 0 to 7
- mu_table: float32 [8], replicated, may hold values from 0.5 to 4
- decay_table: float32 [8], replicated, may hold values from 0.2 to 0.95
- contrast_table: float32 [8], replicated, may hold values from 0.5 to 2
- gravity_kernel: float32 [256, 32, 32], P('lat', 'rad'), may hold values from -1 to 1
Outputs:
- displacement_out: float32 [1024, 32, 2048], P('lat', 'rad')
- memory_out: float32 [1024, 32, 2048], P('lat', 'rad')
- potential: float32 [1024, 32, 2048], P('lat', 'rad')
The draws below stay inside these ranges and needn't reach their ends.
All inputs are finite; a program needn't handle non-finite values.
Results may differ from the reference program's by a relative error of at most 0.0028.
Values sent between devices are 32-bit elements; how exact they have to be, the bound alone decides.
No kernel may reach another device: no remote copies, remote signals or barrier semaphores. Data moves between devices by JAX's collectives and lax.ppermute only.
A program may use at most 64 MiB of HBM per device.

```python
import math
import jax
import jax.numpy as jnp
from jax import lax

NLON = 2048
MODES = 256
NDEG = 256
NMAT = 8
NCLASS = 8
NLAT = 1024
NR = 32


def place_ends(entries, rng, least, top_value):
    spot = [jax.random.randint(jax.random.fold_in(rng, axis), (), 0, length) for axis, length in enumerate(entries.shape)]
    main_axis = entries.shape.index(max(entries.shape))
    neighbour = spot[:main_axis] + [(spot[main_axis] + 1) % entries.shape[main_axis]] + spot[main_axis + 1:]
    return entries.at[tuple(spot)].set(least).at[tuple(neighbour)].set(top_value)


def block_scale(rng, extent, cuts, low, high):
    factor_of, own = 1.0, jax.random.fold_in(rng, 6)
    for position, blocks in cuts:
        draws = jnp.exp(jax.random.uniform(jax.random.fold_in(own, position), (blocks,), jnp.float32, low / len(cuts), high / len(cuts)))
        factor_of = factor_of * jnp.repeat(draws, extent[position] // blocks).reshape([-1 if axis == position else 1 for axis in range(len(extent))])
    return factor_of


def centred(rng, shape, deviation, limit, pieces=(), held_as=jnp.bfloat16):
    values = jax.random.normal(rng, shape, jnp.float32) * deviation
    if len(pieces) > 0:
        values = block_scale(rng, shape, pieces, -0.22, 0.18) * values
    return jnp.clip(values, min=-limit, max=limit).astype(held_as)


def setup_inputs(seed: int = 0) -> dict:
    keys = jax.random.split(jax.random.key(seed), 9)
    return {
        "displacement": centred(keys[0], (NLAT, NR, NLON), 0.5, 3.0, ((0, 64), (1, 8)), jnp.float32),
        "memory": centred(keys[1], (NLAT, NR, NLON), 0.5, 3.0, ((0, 64), (1, 8)), jnp.float32),
        "ice_class": place_ends(jax.random.randint(keys[2], (NLAT, NLON), 0, NCLASS), jax.random.fold_in(keys[2], 1), 0, NCLASS - 1).astype(jnp.int32),
        "material": place_ends(jax.random.randint(keys[3], (NLAT, NR), 0, NMAT), jax.random.fold_in(keys[3], 1), 0, NMAT - 1).astype(jnp.int32),
        "mu_table": jnp.clip(jnp.exp(jax.random.uniform(keys[4], (NMAT,), jnp.float32, math.log(0.5), math.log(4.0))), 0.5, 4.0),
        "decay_table": jnp.clip(jax.random.uniform(keys[5], (NMAT,), jnp.float32, 0.2, 0.95), 0.2, 0.95),
        "contrast_table": jnp.clip(jax.random.uniform(keys[6], (NMAT,), jnp.float32, 0.5, 2.0), 0.5, 2.0),
        "gravity_kernel": centred(keys[7], (NDEG, NR, NR), NR ** -0.5, 1.0, ((0, 64), (1, 8)), jnp.float32),
    }


load_scale = 0.5
kappa_shift = 0.5
relax_factor = 0.8
coupling = 2.0

def lookup(material, table):
    onehot = (material[:, :, None] == jnp.arange(table.shape[0], dtype=jnp.int32)[None, None, :]).astype(jnp.float32)
    return lax.optimization_barrier(jnp.sum(onehot * table[None, None, :], axis=-1))

def fourier_table(nlon, modes):
    longitude = jnp.arange(nlon, dtype=jnp.int32)
    order = jnp.arange(modes, dtype=jnp.int32)
    phase = (longitude[:, None] * order[None, :] % nlon).astype(jnp.float32)
    angle = phase * (2.0 * jnp.pi / nlon)
    scale = jnp.sqrt(jnp.float32(2.0) / nlon)
    return scale * jnp.concatenate([jnp.cos(angle), jnp.sin(angle)], axis=1)

def legendre(cosine, count):

    def step(carry, degree):
        before, current = carry
        nextone = ((2.0 * degree + 1.0) * cosine * current - degree * before) / (degree + 1.0)
        return ((current, nextone), current * jnp.sqrt(degree + 0.5))
    start = (jnp.zeros_like(cosine), jnp.ones_like(cosine))
    _, rows = lax.scan(step, start, jnp.arange(count, dtype=jnp.float32))
    return rows

def sweep(field, memory, source, stiff, decay):
    padded = jnp.pad(field, ((1, 1), (1, 1), (0, 0)))
    beside = padded[2:, 1:-1] + padded[:-2, 1:-1] + padded[1:-1, 2:] + padded[1:-1, :-2]
    beside = beside + jnp.roll(field, 1, axis=2) + jnp.roll(field, -1, axis=2)
    diagonal = stiff * (6.0 + kappa_shift)
    applied = diagonal * field - stiff * beside
    update = relax_factor * (source - memory - applied) / diagonal
    return (field + update, decay * memory + stiff * update)

def reference(displacement, memory, ice_class, material, mu_table, decay_table, contrast_table, gravity_kernel):
    stiff = lookup(material, mu_table)[:, :, None]
    decay = lookup(material, decay_table)[:, :, None]
    contrast = lookup(material, contrast_table)[:, :, None]
    layer_pos = (jnp.arange(NR, dtype=jnp.float32) + 1.0) / NR
    source = load_scale * ice_class.astype(jnp.float32)[:, None, :] * layer_pos[None, :, None]
    field, mem = (displacement, memory)
    for step in range(3):
        field, mem = sweep(field, mem, source, stiff, decay)
    rho = contrast * field
    rho = rho - jnp.sum(rho) / (NLAT * NR * NLON)
    table = fourier_table(NLON, MODES)
    cols = 2 * MODES
    spectra = jnp.dot(rho.reshape(NLAT * NR, NLON), table, precision=lax.Precision.HIGHEST).reshape(NLAT, NR * cols)
    theta = (jnp.arange(NLAT, dtype=jnp.float32) + 0.5) * (jnp.pi / NLAT)
    basis = legendre(jnp.cos(theta), NDEG)
    weighted = basis * (jnp.pi / NLAT * jnp.sin(theta))[None, :]
    coef = jnp.dot(weighted, spectra, precision=lax.Precision.HIGHEST).reshape(NDEG, NR, cols)
    phi = jnp.einsum('nab,nbk->nak', gravity_kernel, coef, precision=lax.Precision.HIGHEST)
    synth = jnp.dot(basis.T, phi.reshape(NDEG, NR * cols), precision=lax.Precision.HIGHEST)
    potential = jnp.dot(synth.reshape(NLAT * NR, cols), table.T, precision=lax.Precision.HIGHEST).reshape(NLAT, NR, NLON)
    loaded = source + coupling * potential
    for step in range(3):
        field, mem = sweep(field, mem, loaded, stiff, decay)
    return (field, mem, potential)
```

```python
import numpy as np
import jax
import jax.numpy as jnp
import ml_dtypes
from jax import lax
from jax.experimental import pallas as pl
from jax.experimental.pallas import tpu as pltpu
from jax.sharding import Mesh
from jax.sharding import PartitionSpec as P

LAT = ("lat_0", "lat_1", "lat_2")
RAD = ("rad_0", "rad_1")
ALL = LAT + RAD

NLON, NLAT, NR, MODES, NDEG = 2048, 1024, 32, 256, 256
DEV, NI, NB, NJ, NK = 512, 64, 8, 16, 4
HALF = NLON // 2
RIN, ROUT = 9, 5
LOAD, SHIFT, RELAX, COUPLE = 0.5, 0.5, 0.8, 2.0
DIAG = 6.0 + SHIFT
F32, BF16 = jnp.float32, jnp.bfloat16


def split_np(x):
    hi = x.astype(np.float32).astype(ml_dtypes.bfloat16)
    lo = (x - hi.astype(np.float64)).astype(np.float32).astype(ml_dtypes.bfloat16)
    return hi, lo


def order_tables():
    kind = np.zeros((2, 2, DEV), np.int64)
    order = np.zeros((2, 2, DEV), np.int64)
    for par in range(2):
        high = [(k, c) for c in range(MODES + par, HALF, 2) for k in (0, 1)]
        rest = iter(high)
        for kk in range(2):
            for p in range(DEV):
                if kk == 0 and p % 2 == par:
                    k, c = (0, p) if p < MODES else (1, p - MODES)
                    if k == 1 and c == 0:
                        k, c = 0, HALF
                else:
                    k, c = next(rest)
                kind[par, kk, p], order[par, kk, p] = k, c
    return kind, order


def fourier_tables():
    kind, order = order_tables()
    l = np.arange(HALF)
    phase = (order[..., None] * l) % NLON
    angle = phase * (2.0 * np.pi / NLON)
    value = np.where(kind[..., None] == 0, np.cos(angle), np.sin(angle)) * np.sqrt(2.0 / NLON)
    value = np.where((order % HALF == 0)[..., None], value * np.sqrt(0.5), value)
    eigen = 2.0 * np.cos(order * (2.0 * np.pi / NLON))
    gain = (1.0 - RELAX) + RELAX / DIAG * eigen
    hi, lo = split_np(value)
    return hi, lo, np.ascontiguousarray(gain.transpose(2, 1, 0).reshape(DEV * 4)).astype(np.float32)


def legendre_tables():
    theta = (np.arange(NLAT) + 0.5) * (np.pi / NLAT)
    mu = np.cos(theta)
    rows = np.zeros((NDEG, NLAT))
    before, current = np.zeros(NLAT), np.ones(NLAT)
    for n in range(NDEG):
        rows[n] = current * np.sqrt(n + 0.5)
        before, current = current, ((2 * n + 1) * mu * current - n * before) / (n + 1)
    weight = np.pi / NLAT * np.sin(theta)
    rows = rows.reshape(NI, 4, NLAT).transpose(1, 0, 2).reshape(NDEG, NI, NJ)
    rows = rows.transpose(0, 2, 1).reshape(NDEG, NLAT)
    weight = weight.reshape(NI, NJ).T.reshape(1, NLAT)
    hi, lo = split_np(rows)
    return hi, lo, weight.astype(np.float32)


def split(x):
    hi = x.astype(BF16)
    return hi, (x - hi.astype(F32)).astype(BF16)


def dot_nt(a, b):
    return lax.dot_general(a, b, (((1,), (1,)), ((), ())), preferred_element_type=F32)


def dot_nn(a, b):
    return lax.dot_general(a, b, (((1,), (0,)), ((), ())), preferred_element_type=F32)


PB = 128


def forward_kernel(u_ref, q_ref, ice_ref, mat_ref, ker_ref, th_ref, tl_ref, a_ref, x_ref, w_ref):
    @pl.when(pl.program_id(0) == 0)
    def _():
        for f, ref in ((0, u_ref), (1, q_ref)):
            for j in range(NJ):
                w_ref[pl.ds(64 * f + 4 * j, 4), :] = ref[j]
        low, high = w_ref[:, :HALF], w_ref[:, HALF:]
        ice = ice_ref[...].astype(F32)
        il, ih = ice[:, :HALF], ice[:, HALF:]
        x_ref[...] = jnp.zeros(x_ref.shape, BF16)
        for k2 in range(2):
            part = low + high if k2 == 0 else low - high
            ipart = il + ih if k2 == 0 else il - ih
            ph, plo = split(part)
            for kk in range(2):
                x_ref[k2, kk, 0:128, :] = plo
                x_ref[k2, kk, 128:256, :] = ph
                x_ref[k2, kk, pl.ds(256 + (kk * 2 + k2) * NJ, NJ), :] = ipart.astype(BF16)

    lane = lax.broadcasted_iota(jnp.int32, (PB, 128), 1)
    first = lane < 64
    extra = jnp.broadcast_to(mat_ref[...], (PB, 128))
    for kk in range(2):
        main = []
        for k2 in range(2):
            x = x_ref[k2, kk]
            r1 = dot_nt(th_ref[k2, kk], x)
            r2 = dot_nt(tl_ref[k2, kk], x[128:])
            main.append(r1[:, 128:256] + (r1[:, :128] + r2[:, :128]))
            extra = extra + (r1[:, 256:] + r2[:, 128:])
        even, odd = main
        a_ref[pl.ds(kk, PB, stride=RIN), :] = jnp.where(first, even, pltpu.roll(odd, 64, 1))
        a_ref[pl.ds(2 + kk, PB, stride=RIN), :] = jnp.where(first, pltpu.roll(even, 64, 1), odd)
    a_ref[pl.ds(4, PB, stride=RIN), :] = extra
    for nn in range(4):
        a_ref[pl.ds(5 + nn, PB, stride=RIN), :] = jnp.broadcast_to(ker_ref[pl.ds(nn, 1), :], (PB, 128))


def forward(u, q, ice, mat, ker, th, tl):
    whole = lambda shape: pl.BlockSpec(shape, lambda g: (0,) * len(shape))
    table = pl.BlockSpec((2, 2, PB, HALF), lambda g: (0, 0, g, 0))
    return pl.pallas_call(
        forward_kernel,
        grid=(DEV // PB,),
        in_specs=[
            whole((NJ, NK, NLON)),
            whole((NJ, NK, NLON)),
            whole((NJ, NLON)),
            whole((1, 128)),
            whole((4, 128)),
            table,
            table,
        ],
        out_specs=pl.BlockSpec((PB * RIN, 128), lambda g: (g, 0)),
        out_shape=jax.ShapeDtypeStruct((DEV * RIN, 128), F32),
        scratch_shapes=[pltpu.VMEM((2, 2, 384, HALF), BF16), pltpu.VMEM((128, NLON), F32)],
        compiler_params=pltpu.CompilerParams(vmem_limit_bytes=48 << 20),
        name="forward",
    )(u, q, ice, mat, ker, th, tl)


def middle_kernel(
    dev_ref, gain_ref, mu_ref, dec_ref, con_ref, b_ref, ph_ref, pl_ref, wt_ref, o_ref,
    u_ref, q_ref, s_ref, st_ref, dc_ref, g_ref, r_ref, z_ref, rt_ref,
):
    p = dev_ref[0]
    par = p % 2
    shape = (NI, 128)
    lane = lax.broadcasted_iota(jnp.int32, shape, 1)
    row = lax.broadcasted_iota(jnp.int32, shape, 0)
    r = lane & 3
    j = (lane >> 2) & 15
    first = lane < 64
    rp = (lane & ~3) | ((lane + 1) & 3)
    rm = (lane & ~3) | ((lane + 3) & 3)
    jp = (lane & 64) | ((lane + 4) & 63)
    jm = (lane & 64) | ((lane + 60) & 63)

    def take(x, index):
        return jnp.take_along_axis(x, index, axis=1)

    zero = jnp.zeros(shape, F32)
    for buf in range(2):
        for kk in range(2):
            u_ref[buf, kk, 0] = zero
            u_ref[buf, kk, NB + 1] = zero
    for b in range(NB):
        extra = b_ref[pl.ds(b * RIN + 4, NI, stride=NB * RIN), :]
        mat = take(extra, 64 + (lane & 63))

        def look(ref):
            out = jnp.full(shape, ref[0], F32)
            for m in range(1, 8):
                out = jnp.where(mat == float(m), ref[m], out)
            return out

        stiff = look(mu_ref)
        st_ref[b] = stiff
        dc_ref[b] = look(dec_ref)
        r_ref[b] = look(con_ref)
        g_ref[b] = (RELAX / DIAG) / stiff
        layer = (r + (4 * b + 1)).astype(F32) * (LOAD / NR)
        for kk in range(2):
            s_ref[kk, b] = take(extra, kk * 32 + (lane >> 2)) * layer
            u_ref[0, kk, b + 1] = b_ref[pl.ds(b * RIN + kk, NI, stride=NB * RIN), :]
            q_ref[kk, b] = b_ref[pl.ds(b * RIN + 2 + kk, NI, stride=NB * RIN), :]

    gains = [jnp.where(first, gain_ref[4 * p + 2 * kk], gain_ref[4 * p + 2 * kk + 1]) for kk in range(2)]

    def sweep(src, dst):
        for kk in range(2):
            for b in range(NB):
                uc = u_ref[src, kk, b + 1]
                up = u_ref[src, kk, b + 2]
                dn = u_ref[src, kk, b]
                ip = jnp.where(row == NI - 1, 0.0, pltpu.roll(uc, NI - 1, 0))
                im = jnp.where(row == 0, 0.0, pltpu.roll(uc, 1, 0))
                beside = take(jnp.where(r == 0, up, uc), rp) + take(jnp.where(r == 3, dn, uc), rm)
                beside = beside + take(jnp.where(j == 0, ip, uc), jp) + take(jnp.where(j == 15, im, uc), jm)
                q = q_ref[kk, b]
                un = gains[kk] * uc + g_ref[b] * (s_ref[kk, b] - q) + (RELAX / DIAG) * beside
                u_ref[dst, kk, b + 1] = un
                q_ref[kk, b] = dc_ref[b] * q + st_ref[b] * (un - uc)

    def three(start):
        def body(step, carry):
            src = (start + step) % 2
            sweep(src, 1 - src)
            return carry

        lax.fori_loop(0, 3, body, 0)

    three(0)
    for h in range(NB // 2):
        pair = [r_ref[2 * h + t] * u_ref[1, 0, 2 * h + t + 1] for t in range(2)]
        rt_ref[:, 128 * h : 128 * h + 128] = jnp.concatenate(pair, axis=0).T
    kept = rt_ref[pl.ds(pl.multiple_of(64 * par, 64), 64), :]
    for jj in range(NJ):
        for b in range(NB):
            z_ref[4 * b : 4 * b + 4, 64 * jj : 64 * jj + 64] = kept[4 * jj : 4 * jj + 4, 64 * b : 64 * b + 64]
    z = z_ref[...]
    mean = jnp.sum(z) * (1.0 / (NLAT * NR))
    z = z - jnp.where(p == 0, mean, 0.0)
    z = z * wt_ref[...]
    z4 = jnp.concatenate([z, z, z, z], axis=0)
    zh, zl = split(z4)
    ph, plo = ph_ref[...], pl_ref[...]
    coef = dot_nt(ph, zh) + (dot_nt(ph, zl) + dot_nt(plo, zh))
    lane1 = lax.broadcasted_iota(jnp.int32, (128, 128), 1)
    sub1 = lax.broadcasted_iota(jnp.int32, (128, 128), 0)
    phi = jnp.zeros((NDEG, 128), F32)
    for b in range(NB):
        prod = jnp.concatenate(
            [
                b_ref[pl.ds(b * RIN + 5 + nn, NI, stride=NB * RIN), :] * coef[64 * nn : 64 * nn + 64]
                for nn in range(4)
            ],
            axis=0,
        )
        pick = (lane1 == (sub1 >> 5) + 4 * b).astype(BF16)
        hi, lo = split(prod)
        phi = phi + (dot_nn(hi, pick) + dot_nn(lo, pick))
    factor = jnp.where(p == 0, 2.0, jnp.where(p == MODES, 0.0, 1.0))
    phi_t = (phi * factor).T[0:NR]
    fh, fl = split(phi_t)
    pot = dot_nn(fh, ph) + (dot_nn(fl, ph) + dot_nn(fh, plo))
    rt_ref[...] = jnp.zeros(rt_ref.shape, F32)
    for jj in range(NJ):
        for b in range(NB):
            z_ref2 = pot[4 * b : 4 * b + 4, 64 * jj : 64 * jj + 64]
            kept_ref = rt_ref.at[pl.ds(pl.multiple_of(64 * par, 64), 64), :]
            kept_ref[4 * jj : 4 * jj + 4, 64 * b : 64 * b + 64] = z_ref2
    for h in range(NB // 2):
        back = rt_ref[:, 128 * h : 128 * h + 128].T
        for t in range(2):
            b = 2 * h + t
            piece = back[64 * t : 64 * t + 64]
            o_ref[pl.ds(b * ROUT + 4, NI, stride=NB * ROUT), :] = piece
            s_ref[0, b] = s_ref[0, b] + COUPLE * piece
    three(1)
    for b in range(NB):
        for kk in range(2):
            o_ref[pl.ds(b * ROUT + kk, NI, stride=NB * ROUT), :] = u_ref[0, kk, b + 1]
            o_ref[pl.ds(b * ROUT + 2 + kk, NI, stride=NB * ROUT), :] = q_ref[kk, b]


def middle(dev, gain, mu, dec, con, b, ph, plo, wt):
    smem = pl.BlockSpec(memory_space=pltpu.SMEM)
    vmem = pl.BlockSpec(memory_space=pltpu.VMEM)
    field = (NB, NI, 128)
    return pl.pallas_call(
        middle_kernel,
        in_specs=[smem] * 5 + [vmem] * 4,
        out_specs=vmem,
        out_shape=jax.ShapeDtypeStruct((DEV * ROUT, 128), F32),
        scratch_shapes=[
            pltpu.VMEM((2, 2, NB + 2, NI, 128), F32),
            pltpu.VMEM((2, *field), F32),
            pltpu.VMEM((2, *field), F32),
            pltpu.VMEM(field, F32),
            pltpu.VMEM(field, F32),
            pltpu.VMEM(field, F32),
            pltpu.VMEM(field, F32),
            pltpu.VMEM((NR, NLAT), F32),
            pltpu.VMEM((128, DEV), F32),
        ],
        compiler_params=pltpu.CompilerParams(vmem_limit_bytes=48 << 20),
        name="middle",
    )(dev, gain, mu, dec, con, b, ph, plo, wt)


LB = 256


def inverse_kernel(b_ref, th_ref, tl_ref, u_ref, q_ref, p_ref, y_ref):
    @pl.when(pl.program_id(0) == 0)
    def _():
        for f in range(3):
            for kk in range(2):
                if f == 2 and kk == 1:
                    continue
                rows = b_ref[pl.ds(4 if f == 2 else 2 * f + kk, DEV, stride=ROUT), :].T
                hi, lo = split(rows)
                for k2 in range(2):
                    y_ref[k2, 64 * f : 64 * f + 64, DEV * kk : DEV * kk + DEV] = hi[64 * k2 : 64 * k2 + 64]
                    y_ref[k2, 192 + 64 * f : 256 + 64 * f, DEV * kk : DEV * kk + DEV] = lo[64 * k2 : 64 * k2 + 64]
        for k2 in range(2):
            for base in (128, 320):
                y_ref[k2, base : base + 64, DEV:] = jnp.zeros((64, DEV), BF16)

    halves = []
    for k2 in range(2):
        th = th_ref[k2].reshape(2 * DEV, LB)
        tl = tl_ref[k2].reshape(2 * DEV, LB)
        y = y_ref[k2]
        r1 = dot_nn(y, th)
        halves.append(r1[:192] + (r1[192:] + dot_nn(y[:192], tl)))
    even, odd = halves
    start = pl.multiple_of(pl.program_id(0) * LB, LB)
    for base, value in ((0, even + odd), (HALF, even - odd)):
        for f, ref in enumerate((u_ref, q_ref, p_ref)):
            for j in range(NJ):
                ref[j, :, pl.ds(base + start, LB)] = value[64 * f + 4 * j : 64 * f + 4 * j + 4]


def inverse(b, th, tl):
    whole = lambda shape: pl.BlockSpec(shape, lambda g: (0,) * len(shape))
    table = pl.BlockSpec((2, 2, DEV, LB), lambda g: (0, 0, 0, g))
    shape = (NJ, NK, NLON)
    return pl.pallas_call(
        inverse_kernel,
        grid=(HALF // LB,),
        in_specs=[whole((DEV * ROUT, 128)), table, table],
        out_specs=[whole(shape)] * 3,
        out_shape=[jax.ShapeDtypeStruct(shape, F32)] * 3,
        scratch_shapes=[pltpu.VMEM((2, 384, HALF), BF16)],
        compiler_params=pltpu.CompilerParams(vmem_limit_bytes=48 << 20),
        name="inverse",
    )(b, th, tl)


def exchange(x, rows):
    x = x.reshape(DEV, rows * 128)
    x = lax.all_to_all(x, ALL, split_axis=0, concat_axis=0, tiled=True)
    return x.reshape(DEV * rows, 128)


def solution(mesh):
    torus = Mesh(mesh.devices.reshape(4, 8, 2, 4, 2), ALL)
    th_np, tl_np, gain_np = fourier_tables()
    ph_np, pl_np, wt_np = legendre_tables()

    def per_device(
        displacement, memory, ice_class, material, mu_table, decay_table, contrast_table, gravity_kernel
    ):
        th, tl = jnp.asarray(th_np), jnp.asarray(tl_np)
        mat = jnp.pad(material.reshape(1, 64).astype(F32), ((0, 0), (64, 0)))
        ker = gravity_kernel.reshape(4, 128)
        dev = lax.axis_index(ALL).reshape(1)
        packed = forward(displacement, memory, ice_class, mat, ker, th, tl)
        arrived = exchange(packed, RIN)
        moved = middle(
            dev, jnp.asarray(gain_np), mu_table, decay_table, contrast_table, arrived,
            jnp.asarray(ph_np), jnp.asarray(pl_np), jnp.asarray(wt_np),
        )
        returned = exchange(moved, ROUT)
        return tuple(inverse(returned, th, tl))

    in_specs = (
        P(LAT, RAD, None),
        P(LAT, RAD, None),
        P(LAT, None),
        P(LAT, RAD),
        P(),
        P(),
        P(),
        P(LAT, RAD, None),
    )
    out_specs = (P(LAT, RAD, None), P(LAT, RAD, None), P(LAT, RAD, None))
    return jax.shard_map(per_device, mesh=torus, in_specs=in_specs, out_specs=out_specs, check_vma=False)
```

```python
import numpy as np
import jax
import jax.numpy as jnp
import ml_dtypes
from jax import lax
from jax.experimental import pallas as pl
from jax.experimental.pallas import tpu as pltpu
from jax.sharding import Mesh
from jax.sharding import PartitionSpec as P

LAT = ("lat_0", "lat_1", "lat_2")
RAD = ("rad_0", "rad_1")
ALL = LAT + RAD

NLON, NLAT, NR, MODES, NDEG = 2048, 1024, 32, 256, 256
DEV, NI, NB, NJ, NK = 512, 64, 8, 16, 4
HALF = NLON // 2
RIN, ROUT = 7, 5
LOAD, SHIFT, RELAX, COUPLE = 0.5, 0.5, 0.8, 2.0
DIAG = 6.0 + SHIFT
F32, BF16 = jnp.float32, jnp.bfloat16


def split_np(x):
    hi = x.astype(np.float32).astype(ml_dtypes.bfloat16)
    lo = (x - hi.astype(np.float64)).astype(np.float32).astype(ml_dtypes.bfloat16)
    return hi, lo


def order_tables():
    kind = np.zeros((2, 2, DEV), np.int64)
    order = np.zeros((2, 2, DEV), np.int64)
    for par in range(2):
        high = [(k, c) for c in range(MODES + par, HALF, 2) for k in (0, 1)]
        rest = iter(high)
        for kk in range(2):
            for p in range(DEV):
                if kk == 0 and p % 2 == par:
                    k, c = (0, p) if p < MODES else (1, p - MODES)
                    if k == 1 and c == 0:
                        k, c = 0, HALF
                else:
                    k, c = next(rest)
                kind[par, kk, p], order[par, kk, p] = k, c
    return kind, order


def fourier_tables():
    kind, order = order_tables()
    l = np.arange(HALF)
    phase = (order[..., None] * l) % NLON
    angle = phase * (2.0 * np.pi / NLON)
    value = np.where(kind[..., None] == 0, np.cos(angle), np.sin(angle)) * np.sqrt(2.0 / NLON)
    value = np.where((order % HALF == 0)[..., None], value * np.sqrt(0.5), value)
    eigen = 2.0 * np.cos(order * (2.0 * np.pi / NLON))
    gain = (1.0 - RELAX) + RELAX / DIAG * eigen
    hi, lo = split_np(value)
    return hi, lo, np.ascontiguousarray(gain.transpose(2, 1, 0).reshape(DEV * 4)).astype(np.float32)


def legendre_tables():
    theta = (np.arange(NLAT) + 0.5) * (np.pi / NLAT)
    mu = np.cos(theta)
    rows = np.zeros((NDEG, NLAT))
    before, current = np.zeros(NLAT), np.ones(NLAT)
    for n in range(NDEG):
        rows[n] = current * np.sqrt(n + 0.5)
        before, current = current, ((2 * n + 1) * mu * current - n * before) / (n + 1)
    weight = np.pi / NLAT * np.sin(theta)
    rows = rows.reshape(NI, 4, NLAT).transpose(1, 0, 2).reshape(NDEG, NI, NJ)
    rows = rows.transpose(0, 2, 1).reshape(NDEG, NLAT)
    weight = weight.reshape(NI, NJ).T.reshape(1, NLAT)
    hi, lo = split_np(rows)
    return hi, lo, weight.astype(np.float32)


def split(x):
    hi = x.astype(BF16)
    return hi, (x - hi.astype(F32)).astype(BF16)


def dot_nt(a, b):
    return lax.dot_general(a, b, (((1,), (1,)), ((), ())), preferred_element_type=F32)


def dot_nn(a, b):
    return lax.dot_general(a, b, (((1,), (0,)), ((), ())), preferred_element_type=F32)


def forward_kernel(
    u_hbm, q_hbm, ice_hbm, mat_ref, ker_ref, th_ref, tl_ref, a_ref, x_ref, w_ref, f_ref, ice_ref, even_ref, extra_ref, sem
):
    g = pl.program_id(0)
    kk, k2 = g // 2, g % 2

    @pl.when(g == 0)
    def _():
        copies = [
            pltpu.make_async_copy(u_hbm, f_ref.at[0], sem.at[0]),
            pltpu.make_async_copy(q_hbm, f_ref.at[1], sem.at[1]),
            pltpu.make_async_copy(ice_hbm, ice_ref, sem.at[2]),
        ]
        for copy in copies:
            copy.start()
        x_ref[:, :, 256:, :] = jnp.zeros((2, 2, 128, HALF), BF16)
        peer = lax.broadcasted_iota(jnp.int32, (DEV, 128), 0)
        core = (peer >> 3) & 1
        for t in range(2):
            mine = jnp.where(core == 0, ker_ref[pl.ds(t, 1), :], ker_ref[pl.ds(2 + t, 1), :])
            a_ref[pl.ds(5 + t, DEV, stride=RIN), :] = mine
        for f in range(2):
            copies[f].wait()
            for j in range(NJ):
                w_ref[pl.ds(64 * f + 4 * j, 4), :] = f_ref[f, j]
        copies[2].wait()
        low, high = w_ref[:, :HALF], w_ref[:, HALF:]
        ice = ice_ref[...].astype(F32)
        il, ih = ice[:, :HALF], ice[:, HALF:]
        for par in range(2):
            part = low + high if par == 0 else low - high
            ipart = il + ih if par == 0 else il - ih
            ph, plo = split(part)
            for slot in range(2):
                x_ref[slot, par, 0:128, :] = plo
                x_ref[slot, par, 128:256, :] = ph
                x_ref[slot, par, pl.ds(256 + (slot * 2 + par) * NJ, NJ), :] = ipart.astype(BF16)
        extra_ref[...] = jnp.broadcast_to(mat_ref[...], (DEV, 128))

    first = lax.broadcasted_iota(jnp.int32, (DEV, 128), 1) < 64
    x = x_ref[kk, k2]
    r1 = dot_nt(th_ref[0, 0], x)
    r2 = dot_nt(tl_ref[0, 0], x[128:])
    main = r1[:, 128:256] + (r1[:, :128] + r2[:, :128])
    extra_ref[...] += r1[:, 256:] + r2[:, 128:]

    @pl.when(k2 == 0)
    def _():
        even_ref[...] = main

    @pl.when(k2 == 1)
    def _():
        even = even_ref[...]
        a_ref[pl.ds(kk, DEV, stride=RIN), :] = jnp.where(first, even, pltpu.roll(main, 64, 1))
        a_ref[pl.ds(2 + kk, DEV, stride=RIN), :] = jnp.where(first, pltpu.roll(even, 64, 1), main)

    @pl.when(g == 3)
    def _():
        a_ref[pl.ds(4, DEV, stride=RIN), :] = extra_ref[...]


def forward(u, q, ice, mat, ker, th, tl):
    whole = lambda shape: pl.BlockSpec(shape, lambda g: (0,) * len(shape))
    hbm = pl.BlockSpec(memory_space=pltpu.MemorySpace.HBM)
    u, q, ice = (pltpu.with_memory_space_constraint(x, pltpu.MemorySpace.HBM) for x in (u, q, ice))
    th, tl = (pltpu.with_memory_space_constraint(x, pltpu.MemorySpace.HBM) for x in (th, tl))
    table = pl.BlockSpec((1, 1, DEV, HALF), lambda g: (g % 2, g // 2, 0, 0))
    return pl.pallas_call(
        forward_kernel,
        grid=(4,),
        in_specs=[hbm, hbm, hbm, whole((1, 128)), whole((4, 128)), table, table],
        out_specs=whole((DEV * RIN, 128)),
        out_shape=jax.ShapeDtypeStruct((DEV * RIN, 128), F32),
        scratch_shapes=[
            pltpu.VMEM((2, 2, 384, HALF), BF16),
            pltpu.VMEM((128, NLON), F32),
            pltpu.VMEM((2, NJ, NK, NLON), F32),
            pltpu.VMEM((NJ, NLON), jnp.int32),
            pltpu.VMEM((DEV, 128), F32),
            pltpu.VMEM((DEV, 128), F32),
            pltpu.SemaphoreType.DMA((3,)),
        ],
        compiler_params=pltpu.CompilerParams(vmem_limit_bytes=48 << 20),
        name="forward",
    )(u, q, ice, mat, ker, th, tl)


def lane_tables():
    shape = (NI, 128)
    lane = lax.broadcasted_iota(jnp.int32, shape, 1)
    row = lax.broadcasted_iota(jnp.int32, shape, 0)
    return shape, lane, row


def take(x, index):
    return jnp.take_along_axis(x, index, axis=1)


def load_materials(b_ref, mu_ref, dec_ref, con_ref, s_ref, st_ref, dc_ref, g_ref, r_ref):
    shape, lane, row = lane_tables()
    r = lane & 3
    for b in range(NB):
        extra = b_ref[pl.ds(b * RIN + 4, NI, stride=NB * RIN), :]
        mat = take(extra, 64 + (lane & 63))

        def look(ref):
            out = jnp.full(shape, ref[0], F32)
            for m in range(1, 8):
                out = jnp.where(mat == float(m), ref[m], out)
            return out

        stiff = look(mu_ref)
        st_ref[b] = stiff
        dc_ref[b] = look(dec_ref)
        if r_ref is not None:
            r_ref[b] = look(con_ref)
        g_ref[b] = (RELAX / DIAG) / stiff
        layer = (r + (4 * b + 1)).astype(F32) * (LOAD / NR)
        for kk in range(2):
            s_ref[kk, b] = take(extra, kk * 32 + (lane >> 2)) * layer


def three_sweeps(p, gain_ref, u_ref, q_ref, s_ref, st_ref, dc_ref, g_ref):
    shape, lane, row = lane_tables()
    r = lane & 3
    j = (lane >> 2) & 15
    rp = (lane & ~3) | ((lane + 1) & 3)
    rm = (lane & ~3) | ((lane + 3) & 3)
    jp = (lane & 64) | ((lane + 4) & 63)
    jm = (lane & 64) | ((lane + 60) & 63)
    gains = [jnp.where(lane < 64, gain_ref[4 * p + 2 * kk], gain_ref[4 * p + 2 * kk + 1]) for kk in range(2)]
    zero = jnp.zeros(shape, F32)
    for buf in range(2):
        for kk in range(2):
            u_ref[buf, kk, 0] = zero
            u_ref[buf, kk, NB + 1] = zero

    def body(step, carry):
        src = step % 2
        dst = 1 - src
        for kk in range(2):
            for b in range(NB):
                uc = u_ref[src, kk, b + 1]
                up = u_ref[src, kk, b + 2]
                dn = u_ref[src, kk, b]
                ip = jnp.where(row == NI - 1, 0.0, pltpu.roll(uc, NI - 1, 0))
                im = jnp.where(row == 0, 0.0, pltpu.roll(uc, 1, 0))
                beside = take(jnp.where(r == 0, up, uc), rp) + take(jnp.where(r == 3, dn, uc), rm)
                beside = beside + take(jnp.where(j == 0, ip, uc), jp) + take(jnp.where(j == 15, im, uc), jm)
                q = q_ref[kk, b]
                un = gains[kk] * uc + g_ref[b] * (s_ref[kk, b] - q) + (RELAX / DIAG) * beside
                u_ref[dst, kk, b + 1] = un
                q_ref[kk, b] = dc_ref[b] * q + st_ref[b] * (un - uc)
        return carry

    lax.fori_loop(0, 3, body, 0)


def half_kernel(b_ref, o_ref):
    for t in range(2):
        o_ref[pl.ds(t * DEV, DEV), :] = b_ref[pl.ds(5 + t, DEV, stride=RIN), :]


def first_kernel(
    dev_ref, gain_ref, mu_ref, dec_ref, con_ref, b_ref, ph_ref, pl_ref, wt_ref, u3_ref, q_ref, c_ref,
    u_ref, s_ref, st_ref, dc_ref, g_ref, r_ref, z_ref, rt_ref,
):
    p = dev_ref[0]
    par = p % 2
    load_materials(b_ref, mu_ref, dec_ref, con_ref, s_ref, st_ref, dc_ref, g_ref, r_ref)
    for b in range(NB):
        for kk in range(2):
            u_ref[0, kk, b + 1] = b_ref[pl.ds(b * RIN + kk, NI, stride=NB * RIN), :]
            q_ref[kk, b] = b_ref[pl.ds(b * RIN + 2 + kk, NI, stride=NB * RIN), :]
    three_sweeps(p, gain_ref, u_ref, q_ref, s_ref, st_ref, dc_ref, g_ref)
    for b in range(NB):
        for kk in range(2):
            u3_ref[kk, b] = u_ref[1, kk, b + 1]
    for h in range(NB // 2):
        pair = [r_ref[2 * h + t] * u_ref[1, 0, 2 * h + t + 1] for t in range(2)]
        rt_ref[:, 128 * h : 128 * h + 128] = jnp.concatenate(pair, axis=0).T
    kept = rt_ref[pl.ds(pl.multiple_of(64 * par, 64), 64), :]
    for jj in range(NJ):
        for b in range(NB):
            z_ref[4 * b : 4 * b + 4, 64 * jj : 64 * jj + 64] = kept[4 * jj : 4 * jj + 4, 64 * b : 64 * b + 64]
    z = z_ref[...]
    mean = jnp.sum(z) * (1.0 / (NLAT * NR))
    z = z - jnp.where(p == 0, mean, 0.0)
    z = z * wt_ref[...]
    z4 = jnp.concatenate([z, z, z, z], axis=0)
    zh, zl = split(z4)
    ph, plo = ph_ref[...], pl_ref[...]
    c_ref[...] = dot_nt(ph, zh) + (dot_nt(ph, zl) + dot_nt(plo, zh))


def second_kernel(
    dev_ref, gain_ref, mu_ref, dec_ref, con_ref, b_ref, ph_ref, pl_ref, u3_ref, q3_ref, c_ref, k_ref, o_ref,
    u_ref, q_ref, s_ref, st_ref, dc_ref, g_ref, rt_ref, phi_ref,
):
    p = dev_ref[0]
    par = p % 2
    core = (p // NB) % 2
    mine = pl.multiple_of(128 * core, 128)
    other = pl.multiple_of(128 - 128 * core, 128)
    load_materials(b_ref, mu_ref, dec_ref, con_ref, s_ref, st_ref, dc_ref, g_ref, None)
    for b in range(NB):
        for kk in range(2):
            u_ref[0, kk, b + 1] = u3_ref[kk, b]
            q_ref[kk, b] = q3_ref[kk, b]
    lane1 = lax.broadcasted_iota(jnp.int32, (128, 128), 1)
    sub1 = lax.broadcasted_iota(jnp.int32, (128, 128), 0)
    phi = jnp.zeros((NDEG, 128), F32)
    coef_mine = c_ref[pl.ds(mine, 128), :]
    coef_other = c_ref[pl.ds(other, 128), :]
    for b in range(NB):
        prod = jnp.concatenate(
            [
                b_ref[pl.ds(b * RIN + 5 + t, NI, stride=NB * RIN), :] * coef_mine[64 * t : 64 * t + 64]
                for t in range(2)
            ]
            + [
                k_ref[pl.ds(t * DEV + b, NI, stride=NB), :] * coef_other[64 * t : 64 * t + 64]
                for t in range(2)
            ],
            axis=0,
        )
        pick = (lane1 == (sub1 >> 5) + 4 * b).astype(BF16)
        hi, lo = split(prod)
        phi = phi + (dot_nn(hi, pick) + dot_nn(lo, pick))
    factor = jnp.where(p == 0, 2.0, jnp.where(p == MODES, 0.0, 1.0))
    phi_ref[pl.ds(mine, 128), :] = phi[:128] * factor
    phi_ref[pl.ds(other, 128), :] = phi[128:] * factor
    fh, fl = split(phi_ref[...].T[0:NR])
    ph, plo = ph_ref[...], pl_ref[...]
    pot = dot_nn(fh, ph) + (dot_nn(fl, ph) + dot_nn(fh, plo))
    rt_ref[...] = jnp.zeros(rt_ref.shape, F32)
    kept_ref = rt_ref.at[pl.ds(pl.multiple_of(64 * par, 64), 64), :]
    for jj in range(NJ):
        for b in range(NB):
            kept_ref[4 * jj : 4 * jj + 4, 64 * b : 64 * b + 64] = pot[4 * b : 4 * b + 4, 64 * jj : 64 * jj + 64]
    for h in range(NB // 2):
        back = rt_ref[:, 128 * h : 128 * h + 128].T
        for t in range(2):
            b = 2 * h + t
            piece = back[64 * t : 64 * t + 64]
            o_ref[pl.ds(b * ROUT + 4, NI, stride=NB * ROUT), :] = piece
            s_ref[0, b] = s_ref[0, b] + COUPLE * piece
    three_sweeps(p, gain_ref, u_ref, q_ref, s_ref, st_ref, dc_ref, g_ref)
    for b in range(NB):
        for kk in range(2):
            o_ref[pl.ds(b * ROUT + kk, NI, stride=NB * ROUT), :] = u_ref[1, kk, b + 1]
            o_ref[pl.ds(b * ROUT + 2 + kk, NI, stride=NB * ROUT), :] = q_ref[kk, b]


FIELD = (NB, NI, 128)


def local_call(kernel, name, scalars, arrays, out_shape, scratch):
    smem = pl.BlockSpec(memory_space=pltpu.SMEM)
    vmem = pl.BlockSpec(memory_space=pltpu.VMEM)
    return pl.pallas_call(
        kernel,
        in_specs=[smem] * len(scalars) + [vmem] * len(arrays),
        out_specs=jax.tree.map(lambda _: vmem, out_shape),
        out_shape=out_shape,
        scratch_shapes=[pltpu.VMEM(shape, F32) for shape in scratch],
        compiler_params=pltpu.CompilerParams(vmem_limit_bytes=48 << 20),
        name=name,
    )(*scalars, *arrays)


LB = 256


def inverse_kernel(b_ref, th_ref, tl_ref, u_ref, q_ref, p_ref, y_ref):
    @pl.when(pl.program_id(0) == 0)
    def _():
        for f in range(3):
            for kk in range(2):
                if f == 2 and kk == 1:
                    continue
                rows = b_ref[pl.ds(4 if f == 2 else 2 * f + kk, DEV, stride=ROUT), :].T
                hi, lo = split(rows)
                for k2 in range(2):
                    y_ref[k2, 64 * f : 64 * f + 64, DEV * kk : DEV * kk + DEV] = hi[64 * k2 : 64 * k2 + 64]
                    y_ref[k2, 192 + 64 * f : 256 + 64 * f, DEV * kk : DEV * kk + DEV] = lo[64 * k2 : 64 * k2 + 64]
        for k2 in range(2):
            for base in (128, 320):
                y_ref[k2, base : base + 64, DEV:] = jnp.zeros((64, DEV), BF16)

    halves = []
    for k2 in range(2):
        th = th_ref[k2].reshape(2 * DEV, LB)
        tl = tl_ref[k2].reshape(2 * DEV, LB)
        y = y_ref[k2]
        r1 = dot_nn(y, th)
        halves.append(r1[:192] + (r1[192:] + dot_nn(y[:192], tl)))
    even, odd = halves
    start = pl.multiple_of(pl.program_id(0) * LB, LB)
    for base, value in ((0, even + odd), (HALF, even - odd)):
        for f, ref in enumerate((u_ref, q_ref, p_ref)):
            for j in range(NJ):
                ref[j, :, pl.ds(base + start, LB)] = value[64 * f + 4 * j : 64 * f + 4 * j + 4]


def inverse(b, th, tl):
    whole = lambda shape: pl.BlockSpec(shape, lambda g: (0,) * len(shape))
    table = pl.BlockSpec((2, 2, DEV, LB), lambda g: (0, 0, 0, g))
    shape = (NJ, NK, NLON)
    return pl.pallas_call(
        inverse_kernel,
        grid=(HALF // LB,),
        in_specs=[whole((DEV * ROUT, 128)), table, table],
        out_specs=[whole(shape)] * 3,
        out_shape=[jax.ShapeDtypeStruct(shape, F32)] * 3,
        scratch_shapes=[pltpu.VMEM((2, 384, HALF), BF16)],
        compiler_params=pltpu.CompilerParams(vmem_limit_bytes=48 << 20),
        name="inverse",
    )(b, th, tl)


def exchange(x, rows):
    x = x.reshape(DEV, rows * 128)
    x = lax.all_to_all(x, ALL, split_axis=0, concat_axis=0, tiled=True)
    return x.reshape(DEV * rows, 128)


def solution(mesh):
    torus = Mesh(mesh.devices.reshape(4, 8, 2, 4, 2), ALL)
    th_np, tl_np, gain_np = fourier_tables()
    ph_np, pl_np, wt_np = legendre_tables()

    def per_device(
        displacement, memory, ice_class, material, mu_table, decay_table, contrast_table, gravity_kernel
    ):
        th, tl = jnp.asarray(th_np), jnp.asarray(tl_np)
        mat = jnp.pad(material.reshape(1, 64).astype(F32), ((0, 0), (64, 0)))
        ker = gravity_kernel.reshape(4, 128)
        dev = lax.axis_index(ALL).reshape(1)
        packed = forward(displacement, memory, ice_class, mat, ker, th, tl)
        arrived = exchange(packed, RIN)
        half = local_call(half_kernel, "half", (), (arrived,), jax.ShapeDtypeStruct((DEV * 2, 128), F32), [])
        swapped = lax.ppermute(half, "lat_2", [(0, 1), (1, 0)])
        scalars = (dev, jnp.asarray(gain_np), mu_table, decay_table, contrast_table)
        ph, plo = jnp.asarray(ph_np), jnp.asarray(pl_np)
        u3, q3, coef = local_call(
            first_kernel, "first", scalars, (arrived, ph, plo, jnp.asarray(wt_np)),
            [
                jax.ShapeDtypeStruct((2, *FIELD), F32),
                jax.ShapeDtypeStruct((2, *FIELD), F32),
                jax.ShapeDtypeStruct((NDEG, 128), F32),
            ],
            [(2, 2, NB + 2, NI, 128), (2, *FIELD), FIELD, FIELD, FIELD, FIELD, (NR, NLAT), (128, DEV)],
        )
        moved = local_call(
            second_kernel, "second", scalars, (arrived, ph, plo, u3, q3, coef, swapped),
            jax.ShapeDtypeStruct((DEV * ROUT, 128), F32),
            [(2, 2, NB + 2, NI, 128), (2, *FIELD), (2, *FIELD), FIELD, FIELD, FIELD, (128, DEV), (NDEG, 128)],
        )
        returned = exchange(moved, ROUT)
        return tuple(inverse(returned, th, tl))

    in_specs = (
        P(LAT, RAD, None),
        P(LAT, RAD, None),
        P(LAT, None),
        P(LAT, RAD),
        P(),
        P(),
        P(),
        P(LAT, RAD, None),
    )
    out_specs = (P(LAT, RAD, None), P(LAT, RAD, None), P(LAT, RAD, None))
    return jax.shard_map(per_device, mesh=torus, in_specs=in_specs, out_specs=out_specs, check_vma=False)
```

```python
import numpy as np
import jax
import jax.numpy as jnp
import ml_dtypes
from jax import lax
from jax.experimental import pallas as pl
from jax.experimental.pallas import tpu as pltpu
from jax.sharding import Mesh
from jax.sharding import PartitionSpec as P

LAT = ("lat_0", "lat_1", "lat_2")
RAD = ("rad_0", "rad_1")
ALL = LAT + RAD

NLON, NLAT, NR, MODES, NDEG = 2048, 1024, 32, 256, 256
DEV, NI, NB, NJ, NK = 512, 64, 8, 16, 4
HALF = NLON // 2
RIN, ROUT = 7, 5
LOAD, SHIFT, RELAX, COUPLE = 0.5, 0.5, 0.8, 2.0
DIAG = 6.0 + SHIFT
F32, BF16 = jnp.float32, jnp.bfloat16


def split_np(x):
    hi = x.astype(np.float32).astype(ml_dtypes.bfloat16)
    lo = (x - hi.astype(np.float64)).astype(np.float32).astype(ml_dtypes.bfloat16)
    return hi, lo


def fourier_tables():
    kind = np.zeros((2, DEV), np.int64)
    order = np.zeros((2, DEV), np.int64)
    for par in range(2):
        rest = iter([(k, c) for c in range(MODES + par, 2 * MODES, 2) for k in (0, 1)])
        for p in range(DEV):
            if p % 2 == par:
                k, c = (0, p) if p < MODES else (1, p - MODES)
            else:
                k, c = next(rest)
            kind[par, p], order[par, p] = k, c
    order[0, MODES] = HALF // 2
    l = np.arange(HALF)
    angle = (order[..., None] * l) % NLON * (2.0 * np.pi / NLON)
    cos, sin = np.cos(angle), np.sin(angle)
    value = np.where(kind[..., None] == 0, cos, sin) * np.sqrt(2.0 / NLON)
    value[0, 0] = np.sqrt(1.0 / NLON)
    value[0, MODES] = (cos[0, MODES] + sin[0, MODES]) * np.sqrt(1.0 / NLON)
    block, t = np.arange(HALF // 2) // 128, np.arange(HALF // 2) % 128
    even = 256 * block + np.where(t % 2 == 0, t, 128 + t - 1)
    odd = 256 * block + np.where(t % 2 == 0, t + 1, 128 + t)
    value = np.stack([value[..., even], value[..., odd]], axis=1)
    eigen = 2.0 * np.cos(order * (2.0 * np.pi / NLON))
    eigen = np.stack([eigen, -eigen])
    gain = (1.0 - RELAX) + RELAX / DIAG * eigen
    hi, lo = split_np(value)
    return hi, lo, np.ascontiguousarray(gain.transpose(2, 0, 1).reshape(DEV * 4)).astype(np.float32)


def legendre_tables():
    theta = (np.arange(NLAT) + 0.5) * (np.pi / NLAT)
    mu = np.cos(theta)
    rows = np.zeros((NDEG, NLAT))
    before, current = np.zeros(NLAT), np.ones(NLAT)
    for n in range(NDEG):
        rows[n] = current * np.sqrt(n + 0.5)
        before, current = current, ((2 * n + 1) * mu * current - n * before) / (n + 1)
    weight = np.pi / NLAT * np.sin(theta)
    rows = rows.reshape(NI, 4, NLAT).transpose(1, 0, 2).reshape(NDEG, NI, NJ)
    rows = rows.transpose(0, 2, 1).reshape(NDEG, NLAT)
    weight = weight.reshape(NI, NJ).T.reshape(1, NLAT)
    hi, lo = split_np(rows)
    return hi, lo, weight.astype(np.float32)


def split(x):
    hi = x.astype(BF16)
    return hi, (x - hi.astype(F32)).astype(BF16)


def dot_nt(a, b):
    return lax.dot_general(a, b, (((1,), (1,)), ((), ())), preferred_element_type=F32)


def dot_nn(a, b):
    return lax.dot_general(a, b, (((1,), (0,)), ((), ())), preferred_element_type=F32)


QUART = HALF // 2


def forward_kernel(
    u_hbm, q_hbm, ice_hbm, th_hbm, tl_hbm, mat_ref, ker_ref, a_ref, x_ref, w_ref, f_ref, ice_ref, th_ref, tl_ref, sem
):
    copies = [
        pltpu.make_async_copy(u_hbm, f_ref.at[0], sem.at[0]),
        pltpu.make_async_copy(q_hbm, f_ref.at[1], sem.at[1]),
        pltpu.make_async_copy(ice_hbm, ice_ref, sem.at[2]),
    ]
    for k2 in range(2):
        for e in range(2):
            n = 3 + 4 * k2 + 2 * e
            copies.append(pltpu.make_async_copy(th_hbm.at[k2, e], th_ref.at[k2, e], sem.at[n]))
            copies.append(pltpu.make_async_copy(tl_hbm.at[k2, e], tl_ref.at[k2, e], sem.at[n + 1]))
    for copy in copies:
        copy.start()
    peer = lax.broadcasted_iota(jnp.int32, (DEV, 128), 0)
    lane = lax.broadcasted_iota(jnp.int32, (DEV, 128), 1)
    core = (peer >> 3) & 1
    ker = jnp.concatenate([ker_ref[:, rr, :] for rr in range(NK)], axis=1)
    for t in range(2):
        a_ref[pl.ds(5 + t, DEV, stride=RIN), :] = jnp.where(core == 0, ker[t : t + 1], ker[2 + t : 3 + t])
    place = lax.broadcasted_iota(jnp.int32, (NJ, 128), 0)
    column = lax.broadcasted_iota(jnp.int32, (NJ, 128), 1)
    spread = ((column >> 2) == place + NJ).astype(BF16)
    mat = dot_nn(mat_ref[...].astype(F32).astype(BF16), spread)
    mat = jnp.where((lane[:NK] & 3) == peer[:NK], mat, 0.0)
    extra = jnp.broadcast_to(jnp.sum(mat, axis=0, keepdims=True), (DEV, 128))
    x_ref[:, :, 256:, :] = jnp.zeros((2, 2, 128, QUART), BF16)
    for f in range(2):
        copies[f].wait()
        for j in range(NJ):
            w_ref[pl.ds(64 * f + 4 * j, 4), :] = f_ref[f, j]
    copies[2].wait()
    w_ref[pl.ds(128, NJ), :] = ice_ref[...].astype(F32)
    rows = 128 + NJ
    parity = lax.broadcasted_iota(jnp.int32, (rows, 128), 1) & 1
    for m in range(HALF // 256):
        parts = []
        for t in range(2):
            start = 256 * m + 128 * t
            low, high = w_ref[:, start : start + 128], w_ref[:, HALF + start : HALF + start + 128]
            parts.append((low + high, low - high))
        for k2 in range(2):
            v0, v1 = parts[0][k2], parts[1][k2]
            for e, value in (
                (0, jnp.where(parity == 0, v0, pltpu.roll(v1, 1, 1))),
                (1, jnp.where(parity == 0, pltpu.roll(v0, 127, 1), v1)),
            ):
                hi, lo = split(value[:128])
                cols = slice(128 * m, 128 * m + 128)
                x_ref[k2, e, 0:128, cols] = lo
                x_ref[k2, e, 128:256, cols] = hi
                x_ref[k2, e, 256 + NJ * k2 : 256 + NJ * k2 + NJ, cols] = value[128:].astype(BF16)
    first = lane < 64
    slots = []
    ice_sum = [0.0, 0.0]
    for k2 in range(2):
        product = []
        for e in range(2):
            n = 3 + 4 * k2 + 2 * e
            copies[n].wait()
            copies[n + 1].wait()
            x = x_ref[k2, e]
            r1 = dot_nt(th_ref[k2, e], x)
            r2 = dot_nt(tl_ref[k2, e], x[128:])
            product.append(r1[:, 128:256] + (r1[:, :128] + r2[:, :128]))
            ice_sum[e] = ice_sum[e] + (r1[:, 256:] + r2[:, 128:])
        slots.append((product[0] + product[1], product[0] - product[1]))
    for kk in range(2):
        even, odd = slots[0][kk], slots[1][kk]
        a_ref[pl.ds(kk, DEV, stride=RIN), :] = jnp.where(first, even, pltpu.roll(odd, 64, 1))
        a_ref[pl.ds(2 + kk, DEV, stride=RIN), :] = jnp.where(first, pltpu.roll(even, 64, 1), odd)
    extra = extra + (ice_sum[0] + ice_sum[1]) + pltpu.roll(ice_sum[0] - ice_sum[1], 32, 1)
    a_ref[pl.ds(4, DEV, stride=RIN), :] = extra


def forward(u, q, ice, mat, ker, th, tl):
    hbm = pl.BlockSpec(memory_space=pltpu.MemorySpace.HBM)
    vmem = pl.BlockSpec(memory_space=pltpu.VMEM)
    far = [pltpu.with_memory_space_constraint(x, pltpu.MemorySpace.HBM) for x in (u, q, ice, th, tl)]
    return pl.pallas_call(
        forward_kernel,
        in_specs=[hbm] * 5 + [vmem] * 2,
        out_specs=vmem,
        out_shape=jax.ShapeDtypeStruct((DEV * RIN, 128), F32),
        scratch_shapes=[
            pltpu.VMEM((2, 2, 384, QUART), BF16),
            pltpu.VMEM((128 + NJ, NLON), F32),
            pltpu.VMEM((2, NJ, NK, NLON), F32),
            pltpu.VMEM((NJ, NLON), jnp.int32),
            pltpu.VMEM((2, 2, DEV, QUART), BF16),
            pltpu.VMEM((2, 2, DEV, QUART), BF16),
            pltpu.SemaphoreType.DMA((11,)),
        ],
        compiler_params=pltpu.CompilerParams(vmem_limit_bytes=48 << 20),
        name="forward",
    )(*far, mat, ker)


def lane_tables():
    shape = (NI, 128)
    lane = lax.broadcasted_iota(jnp.int32, shape, 1)
    row = lax.broadcasted_iota(jnp.int32, shape, 0)
    return shape, lane, row


def take(x, index):
    return jnp.take_along_axis(x, index, axis=1)


def load_materials(b_ref, mu_ref, dec_ref, con_ref, s_ref, st_ref, dc_ref, g_ref, r_ref):
    shape, lane, row = lane_tables()
    r = lane & 3
    for b in range(NB):
        extra = b_ref[pl.ds(b * RIN + 4, NI, stride=NB * RIN), :]
        mat = take(extra, 64 + (lane & 63))

        def look(ref):
            out = jnp.full(shape, ref[0], F32)
            for m in range(1, 8):
                out = jnp.where(mat == float(m), ref[m], out)
            return out

        stiff = look(mu_ref)
        st_ref[b] = stiff
        dc_ref[b] = look(dec_ref)
        if r_ref is not None:
            r_ref[b] = look(con_ref)
        g_ref[b] = (RELAX / DIAG) / stiff
        layer = (r + (4 * b + 1)).astype(F32) * (LOAD / NR)
        for kk in range(2):
            s_ref[kk, b] = take(extra, kk * 32 + (lane >> 2)) * layer


def three_sweeps(p, gain_ref, u_ref, q_ref, s_ref, st_ref, dc_ref, g_ref):
    shape, lane, row = lane_tables()
    r = lane & 3
    j = (lane >> 2) & 15
    rp = (lane & ~3) | ((lane + 1) & 3)
    rm = (lane & ~3) | ((lane + 3) & 3)
    jp = (lane & 64) | ((lane + 4) & 63)
    jm = (lane & 64) | ((lane + 60) & 63)
    gains = [jnp.where(lane < 64, gain_ref[4 * p + 2 * kk], gain_ref[4 * p + 2 * kk + 1]) for kk in range(2)]
    zero = jnp.zeros(shape, F32)
    for buf in range(2):
        for kk in range(2):
            u_ref[buf, kk, 0] = zero
            u_ref[buf, kk, NB + 1] = zero

    for step in range(3):
        src, dst = step % 2, 1 - step % 2
        for kk in range(2):
            for b in range(NB):
                uc = u_ref[src, kk, b + 1]
                up = u_ref[src, kk, b + 2]
                dn = u_ref[src, kk, b]
                ip = jnp.where(row == NI - 1, 0.0, pltpu.roll(uc, NI - 1, 0))
                im = jnp.where(row == 0, 0.0, pltpu.roll(uc, 1, 0))
                beside = take(jnp.where(r == 0, up, uc), rp) + take(jnp.where(r == 3, dn, uc), rm)
                beside = beside + take(jnp.where(j == 0, ip, uc), jp) + take(jnp.where(j == 15, im, uc), jm)
                q = q_ref[kk, b]
                un = gains[kk] * uc + g_ref[b] * (s_ref[kk, b] - q) + (RELAX / DIAG) * beside
                u_ref[dst, kk, b + 1] = un
                q_ref[kk, b] = dc_ref[b] * q + st_ref[b] * (un - uc)


def half_kernel(b_ref, o_ref):
    for t in range(2):
        o_ref[pl.ds(t * DEV, DEV), :] = b_ref[pl.ds(5 + t, DEV, stride=RIN), :]


def first_kernel(
    dev_ref, gain_ref, mu_ref, dec_ref, con_ref, b_ref, ph_ref, pl_ref, wt_ref, u3_ref, q_ref, c_ref,
    u_ref, s_ref, st_ref, dc_ref, g_ref, r_ref, z_ref, rt_ref,
):
    p = dev_ref[0]
    par = p % 2
    load_materials(b_ref, mu_ref, dec_ref, con_ref, s_ref, st_ref, dc_ref, g_ref, r_ref)
    for b in range(NB):
        for kk in range(2):
            u_ref[0, kk, b + 1] = b_ref[pl.ds(b * RIN + kk, NI, stride=NB * RIN), :]
            q_ref[kk, b] = b_ref[pl.ds(b * RIN + 2 + kk, NI, stride=NB * RIN), :]
    three_sweeps(p, gain_ref, u_ref, q_ref, s_ref, st_ref, dc_ref, g_ref)
    for b in range(NB):
        for kk in range(2):
            u3_ref[kk, b] = u_ref[1, kk, b + 1]
    for h in range(NB // 2):
        pair = [r_ref[2 * h + t] * u_ref[1, 0, 2 * h + t + 1] for t in range(2)]
        rt_ref[:, 128 * h : 128 * h + 128] = jnp.concatenate(pair, axis=0).T
    kept = rt_ref[pl.ds(pl.multiple_of(64 * par, 64), 64), :]
    for jj in range(NJ):
        for b in range(NB):
            z_ref[4 * b : 4 * b + 4, 64 * jj : 64 * jj + 64] = kept[4 * jj : 4 * jj + 4, 64 * b : 64 * b + 64]
    z = z_ref[...]
    mean = jnp.sum(z) * (1.0 / (NLAT * NR))
    z = z - jnp.where(p == 0, mean, 0.0)
    z = z * wt_ref[...]
    z4 = jnp.concatenate([z, z, z, z], axis=0)
    zh, zl = split(z4)
    ph, plo = ph_ref[...], pl_ref[...]
    c_ref[...] = dot_nt(ph, zh) + (dot_nt(ph, zl) + dot_nt(plo, zh))


def second_kernel(
    dev_ref, gain_ref, mu_ref, dec_ref, con_ref, b_ref, ph_ref, pl_ref, u3_ref, q3_ref, c_ref, k_ref, o_ref,
    u_ref, q_ref, s_ref, st_ref, dc_ref, g_ref, rt_ref, phi_ref,
):
    p = dev_ref[0]
    par = p % 2
    core = (p // NB) % 2
    mine = pl.multiple_of(128 * core, 128)
    other = pl.multiple_of(128 - 128 * core, 128)
    load_materials(b_ref, mu_ref, dec_ref, con_ref, s_ref, st_ref, dc_ref, g_ref, None)
    for b in range(NB):
        for kk in range(2):
            u_ref[0, kk, b + 1] = u3_ref[kk, b]
            q_ref[kk, b] = q3_ref[kk, b]
    lane1 = lax.broadcasted_iota(jnp.int32, (128, 128), 1)
    sub1 = lax.broadcasted_iota(jnp.int32, (128, 128), 0)
    phi = jnp.zeros((NDEG, 128), F32)
    coef_mine = c_ref[pl.ds(mine, 128), :]
    coef_other = c_ref[pl.ds(other, 128), :]
    for b in range(NB):
        prod = jnp.concatenate(
            [
                b_ref[pl.ds(b * RIN + 5 + t, NI, stride=NB * RIN), :] * coef_mine[64 * t : 64 * t + 64]
                for t in range(2)
            ]
            + [
                k_ref[pl.ds(t * DEV + b, NI, stride=NB), :] * coef_other[64 * t : 64 * t + 64]
                for t in range(2)
            ],
            axis=0,
        )
        pick = (lane1 == (sub1 >> 5) + 4 * b).astype(BF16)
        hi, lo = split(prod)
        phi = phi + (dot_nn(hi, pick) + dot_nn(lo, pick))
    factor = jnp.where(p == 0, 2.0, jnp.where(p == MODES, 0.0, 1.0))
    phi_ref[pl.ds(mine, 128), :] = phi[:128] * factor
    phi_ref[pl.ds(other, 128), :] = phi[128:] * factor
    fh, fl = split(phi_ref[...].T[0:NR])
    ph, plo = ph_ref[...], pl_ref[...]
    pot = dot_nn(fh, ph) + (dot_nn(fl, ph) + dot_nn(fh, plo))
    rt_ref[...] = jnp.zeros(rt_ref.shape, F32)
    kept_ref = rt_ref.at[pl.ds(pl.multiple_of(64 * par, 64), 64), :]
    for jj in range(NJ):
        for b in range(NB):
            kept_ref[4 * jj : 4 * jj + 4, 64 * b : 64 * b + 64] = pot[4 * b : 4 * b + 4, 64 * jj : 64 * jj + 64]
    for h in range(NB // 2):
        back = rt_ref[:, 128 * h : 128 * h + 128].T
        for t in range(2):
            b = 2 * h + t
            piece = back[64 * t : 64 * t + 64]
            o_ref[pl.ds(b * ROUT + 4, NI, stride=NB * ROUT), :] = piece
            s_ref[0, b] = s_ref[0, b] + COUPLE * piece
    three_sweeps(p, gain_ref, u_ref, q_ref, s_ref, st_ref, dc_ref, g_ref)
    for b in range(NB):
        for kk in range(2):
            o_ref[pl.ds(b * ROUT + kk, NI, stride=NB * ROUT), :] = u_ref[1, kk, b + 1]
            o_ref[pl.ds(b * ROUT + 2 + kk, NI, stride=NB * ROUT), :] = q_ref[kk, b]


FIELD = (NB, NI, 128)


def local_call(kernel, name, scalars, arrays, out_shape, scratch):
    smem = pl.BlockSpec(memory_space=pltpu.SMEM)
    vmem = pl.BlockSpec(memory_space=pltpu.VMEM)
    return pl.pallas_call(
        kernel,
        in_specs=[smem] * len(scalars) + [vmem] * len(arrays),
        out_specs=jax.tree.map(lambda _: vmem, out_shape),
        out_shape=out_shape,
        scratch_shapes=[pltpu.VMEM(shape, F32) for shape in scratch],
        compiler_params=pltpu.CompilerParams(vmem_limit_bytes=48 << 20),
        name=name,
    )(*scalars, *arrays)


def inverse_kernel(b_ref, th_ref, tl_ref, u_hbm, q_hbm, p_hbm, y_ref, out_ref, sem):
    for f in range(3):
        slot = [b_ref[pl.ds(4 if f == 2 else 2 * f + kk, DEV, stride=ROUT), :] for kk in range(1 if f == 2 else 2)]
        pair = [slot[0].T] * 2 if f == 2 else [(slot[0] + slot[1]).T, (slot[0] - slot[1]).T]
        for e in range(2):
            hi, lo = split(pair[e])
            for k2 in range(2):
                y_ref[k2, e, 64 * f : 64 * f + 64, :] = hi[64 * k2 : 64 * k2 + 64]
                y_ref[k2, e, 192 + 64 * f : 256 + 64 * f, :] = lo[64 * k2 : 64 * k2 + 64]
    parity = lax.broadcasted_iota(jnp.int32, (192, 128), 1) & 1
    copies = []
    for n in range(2):
        cols = slice(256 * n, 256 * n + 256)
        halves = []
        for k2 in range(2):
            made = []
            for e in range(2):
                y = y_ref[k2, e]
                th, tl = th_ref[k2, e, :, cols], tl_ref[k2, e, :, cols]
                r1 = dot_nn(y, th)
                made.append(r1[:192] + (r1[192:] + dot_nn(y[:192], tl)))
            halves.append(made)
        for t in range(2):
            m = 2 * n + t
            both = []
            for k2 in range(2):
                even, odd = (x[:, 128 * t : 128 * t + 128] for x in halves[k2])
                both.append(
                    (
                        jnp.where(parity == 0, even, pltpu.roll(odd, 1, 1)),
                        jnp.where(parity == 0, pltpu.roll(even, 127, 1), odd),
                    )
                )
            for v in range(2):
                for base, value in ((0, both[0][v] + both[1][v]), (HALF, both[0][v] - both[1][v])):
                    start = base + 256 * m + 128 * v
                    for f in range(3):
                        for j in range(NJ):
                            row = 64 * f + 4 * j
                            out_ref[f, j, :, start : start + 128] = value[row : row + 4]
        for f, ref in enumerate((u_hbm, q_hbm, p_hbm)):
            for h in range(2):
                span = pl.ds(HALF * h + 512 * n, 512)
                copy = pltpu.make_async_copy(out_ref.at[f, :, :, span], ref.at[:, :, span], sem.at[n, f, h])
                copy.start()
                copies.append(copy)
    for copy in copies:
        copy.wait()


def inverse(b, th, tl):
    hbm = pl.BlockSpec(memory_space=pltpu.MemorySpace.HBM)
    vmem = pl.BlockSpec(memory_space=pltpu.VMEM)
    shape = (NJ, NK, NLON)
    return pl.pallas_call(
        inverse_kernel,
        in_specs=[vmem] * 3,
        out_specs=[hbm] * 3,
        out_shape=[jax.ShapeDtypeStruct(shape, F32)] * 3,
        scratch_shapes=[
            pltpu.VMEM((2, 2, 384, DEV), BF16),
            pltpu.VMEM((3, *shape), F32),
            pltpu.SemaphoreType.DMA((2, 3, 2)),
        ],
        compiler_params=pltpu.CompilerParams(vmem_limit_bytes=48 << 20),
        name="inverse",
    )(b, th, tl)


def exchange(x, rows):
    x = x.reshape(DEV, rows * 128)
    x = lax.all_to_all(x, ALL, split_axis=0, concat_axis=0, tiled=True)
    return x.reshape(DEV * rows, 128)


def solution(mesh):
    torus = Mesh(mesh.devices.reshape(4, 8, 2, 4, 2), ALL)
    th_np, tl_np, gain_np = fourier_tables()
    ph_np, pl_np, wt_np = legendre_tables()

    def per_device(
        displacement, memory, ice_class, material, mu_table, decay_table, contrast_table, gravity_kernel
    ):
        th, tl = jnp.asarray(th_np), jnp.asarray(tl_np)
        dev = lax.axis_index(ALL).reshape(1)
        packed = forward(displacement, memory, ice_class, material.T, gravity_kernel, th, tl)
        arrived = exchange(packed, RIN)
        half = local_call(half_kernel, "half", (), (arrived,), jax.ShapeDtypeStruct((DEV * 2, 128), F32), [])
        swapped = lax.ppermute(half, "lat_2", [(0, 1), (1, 0)])
        scalars = (dev, jnp.asarray(gain_np), mu_table, decay_table, contrast_table)
        ph, plo = jnp.asarray(ph_np), jnp.asarray(pl_np)
        u3, q3, coef = local_call(
            first_kernel, "first", scalars, (arrived, ph, plo, jnp.asarray(wt_np)),
            [
                jax.ShapeDtypeStruct((2, *FIELD), F32),
                jax.ShapeDtypeStruct((2, *FIELD), F32),
                jax.ShapeDtypeStruct((NDEG, 128), F32),
            ],
            [(2, 2, NB + 2, NI, 128), (2, *FIELD), FIELD, FIELD, FIELD, FIELD, (NR, NLAT), (128, DEV)],
        )
        moved = local_call(
            second_kernel, "second", scalars, (arrived, ph, plo, u3, q3, coef, swapped),
            jax.ShapeDtypeStruct((DEV * ROUT, 128), F32),
            [(2, 2, NB + 2, NI, 128), (2, *FIELD), (2, *FIELD), FIELD, FIELD, FIELD, (128, DEV), (NDEG, 128)],
        )
        returned = exchange(moved, ROUT)
        return tuple(inverse(returned, th, tl))

    in_specs = (
        P(LAT, RAD, None),
        P(LAT, RAD, None),
        P(LAT, None),
        P(LAT, RAD),
        P(),
        P(),
        P(),
        P(LAT, RAD, None),
    )
    out_specs = (P(LAT, RAD, None), P(LAT, RAD, None), P(LAT, RAD, None))
    return jax.shard_map(per_device, mesh=torus, in_specs=in_specs, out_specs=out_specs, check_vma=False)
```

```python
import numpy as np
import jax
import jax.numpy as jnp
import ml_dtypes
from jax import lax
from jax.experimental import pallas as pl
from jax.experimental.pallas import tpu as pltpu
from jax.sharding import Mesh
from jax.sharding import PartitionSpec as P

LAT = ("lat_0", "lat_1", "lat_2")
RAD = ("rad_0", "rad_1")
ALL = LAT + RAD

NLON, NLAT, NR, MODES, NDEG = 2048, 1024, 32, 256, 256
DEV, NI, NB, NJ, NK = 512, 64, 8, 16, 4
HALF = NLON // 2
RIN, ROUT = 7, 5
LOAD, SHIFT, RELAX, COUPLE = 0.5, 0.5, 0.8, 2.0
DIAG = 6.0 + SHIFT
F32, BF16 = jnp.float32, jnp.bfloat16


def split_np(x):
    hi = x.astype(np.float32).astype(ml_dtypes.bfloat16)
    lo = (x - hi.astype(np.float64)).astype(np.float32).astype(ml_dtypes.bfloat16)
    return hi, lo


def fourier_tables():
    kind = np.zeros((2, DEV), np.int64)
    order = np.zeros((2, DEV), np.int64)
    for par in range(2):
        rest = iter([(k, c) for c in range(MODES + par, 2 * MODES, 2) for k in (0, 1)])
        for p in range(DEV):
            if p % 2 == par:
                k, c = (0, p) if p < MODES else (1, p - MODES)
            else:
                k, c = next(rest)
            kind[par, p], order[par, p] = k, c
    order[0, MODES] = HALF // 2
    l = np.arange(HALF)
    angle = (order[..., None] * l) % NLON * (2.0 * np.pi / NLON)
    cos, sin = np.cos(angle), np.sin(angle)
    value = np.where(kind[..., None] == 0, cos, sin) * np.sqrt(2.0 / NLON)
    value[0, 0] = np.sqrt(1.0 / NLON)
    value[0, MODES] = (cos[0, MODES] + sin[0, MODES]) * np.sqrt(1.0 / NLON)
    block, t = np.arange(HALF // 2) // 128, np.arange(HALF // 2) % 128
    even = 256 * block + np.where(t % 2 == 0, t, 128 + t - 1)
    odd = 256 * block + np.where(t % 2 == 0, t + 1, 128 + t)
    value = np.stack([value[..., even], value[..., odd]], axis=1)
    eigen = 2.0 * np.cos(order * (2.0 * np.pi / NLON))
    eigen = np.stack([eigen, -eigen])
    gain = (1.0 - RELAX) + RELAX / DIAG * eigen
    hi, lo = split_np(value)
    return hi, lo, np.ascontiguousarray(gain.transpose(2, 0, 1).reshape(DEV * 4)).astype(np.float32)


def legendre_tables():
    theta = (np.arange(NLAT) + 0.5) * (np.pi / NLAT)
    mu = np.cos(theta)
    rows = np.zeros((NDEG, NLAT))
    before, current = np.zeros(NLAT), np.ones(NLAT)
    for n in range(NDEG):
        rows[n] = current * np.sqrt(n + 0.5)
        before, current = current, ((2 * n + 1) * mu * current - n * before) / (n + 1)
    weight = np.pi / NLAT * np.sin(theta)
    rows = rows.reshape(NI, 4, NLAT).transpose(1, 0, 2).reshape(NDEG, NI, NJ)
    rows = rows.transpose(0, 2, 1).reshape(NDEG, NLAT)
    weight = weight.reshape(NI, NJ).T.reshape(1, NLAT)
    hi, lo = split_np(rows)
    return hi, lo, weight.astype(np.float32)


def split(x):
    hi = x.astype(BF16)
    return hi, (x - hi.astype(F32)).astype(BF16)


def dot_nt(a, b):
    return lax.dot_general(a, b, (((1,), (1,)), ((), ())), preferred_element_type=F32)


def dot_nn(a, b):
    return lax.dot_general(a, b, (((1,), (0,)), ((), ())), preferred_element_type=F32)


QUART = HALF // 2


def forward_kernel(
    u_hbm, q_hbm, ice_hbm, mat_hbm, ker_hbm, th_hbm, tl_hbm, a_ref,
    x_ref, w_ref, f_ref, ice_ref, mat_ref, ker_ref, th_ref, tl_ref, sem,
):
    copies = [
        pltpu.make_async_copy(u_hbm, f_ref.at[0], sem.at[0]),
        pltpu.make_async_copy(q_hbm, f_ref.at[1], sem.at[1]),
        pltpu.make_async_copy(ice_hbm, ice_ref, sem.at[2]),
        pltpu.make_async_copy(mat_hbm, mat_ref, sem.at[3]),
        pltpu.make_async_copy(ker_hbm, ker_ref, sem.at[4]),
    ]
    for k2 in range(2):
        for e in range(2):
            n = 5 + 4 * k2 + 2 * e
            copies.append(pltpu.make_async_copy(th_hbm.at[k2, e], th_ref.at[k2, e], sem.at[n]))
            copies.append(pltpu.make_async_copy(tl_hbm.at[k2, e], tl_ref.at[k2, e], sem.at[n + 1]))
    for copy in copies:
        copy.start()
    peer = lax.broadcasted_iota(jnp.int32, (DEV, 128), 0)
    lane = lax.broadcasted_iota(jnp.int32, (DEV, 128), 1)
    core = (peer >> 3) & 1
    x_ref[:, :, 256:, :] = jnp.zeros((2, 2, 128, QUART), BF16)
    copies[3].wait()
    copies[4].wait()
    ker = jnp.concatenate([ker_ref[:, rr, :] for rr in range(NK)], axis=1)
    for t in range(2):
        a_ref[pl.ds(5 + t, DEV, stride=RIN), :] = jnp.where(core == 0, ker[t : t + 1], ker[2 + t : 3 + t])
    place = lax.broadcasted_iota(jnp.int32, (NJ, 128), 0)
    column = lax.broadcasted_iota(jnp.int32, (NJ, 128), 1)
    spread = ((column >> 2) == place + NJ).astype(BF16)
    mat = dot_nn(mat_ref[...].astype(F32).astype(BF16), spread)
    mat = jnp.where((lane[:NK] & 3) == peer[:NK], mat, 0.0)
    extra = jnp.broadcast_to(jnp.sum(mat, axis=0, keepdims=True), (DEV, 128))
    for f in range(2):
        copies[f].wait()
        for j in range(NJ):
            w_ref[pl.ds(64 * f + 4 * j, 4), :] = f_ref[f, j]
    copies[2].wait()
    w_ref[pl.ds(128, NJ), :] = ice_ref[...].astype(F32)
    rows = 128 + NJ
    parity = lax.broadcasted_iota(jnp.int32, (rows, 128), 1) & 1
    for m in range(HALF // 256):
        parts = []
        for t in range(2):
            start = 256 * m + 128 * t
            low, high = w_ref[:, start : start + 128], w_ref[:, HALF + start : HALF + start + 128]
            parts.append((low + high, low - high))
        for k2 in range(2):
            v0, v1 = parts[0][k2], parts[1][k2]
            for e, value in (
                (0, jnp.where(parity == 0, v0, pltpu.roll(v1, 1, 1))),
                (1, jnp.where(parity == 0, pltpu.roll(v0, 127, 1), v1)),
            ):
                hi, lo = split(value[:128])
                cols = slice(128 * m, 128 * m + 128)
                x_ref[k2, e, 0:128, cols] = lo
                x_ref[k2, e, 128:256, cols] = hi
                x_ref[k2, e, 256 + NJ * k2 : 256 + NJ * k2 + NJ, cols] = value[128:].astype(BF16)
    first = lane < 64
    slots = []
    ice_sum = [0.0, 0.0]
    for k2 in range(2):
        product = []
        for e in range(2):
            n = 5 + 4 * k2 + 2 * e
            copies[n].wait()
            copies[n + 1].wait()
            x = x_ref[k2, e]
            r1 = dot_nt(th_ref[k2, e], x)
            r2 = dot_nt(tl_ref[k2, e], x[128:])
            product.append(r1[:, 128:256] + (r1[:, :128] + r2[:, :128]))
            ice_sum[e] = ice_sum[e] + (r1[:, 256:] + r2[:, 128:])
        slots.append((product[0] + product[1], product[0] - product[1]))
    for kk in range(2):
        even, odd = slots[0][kk], slots[1][kk]
        a_ref[pl.ds(kk, DEV, stride=RIN), :] = jnp.where(first, even, pltpu.roll(odd, 64, 1))
        a_ref[pl.ds(2 + kk, DEV, stride=RIN), :] = jnp.where(first, pltpu.roll(even, 64, 1), odd)
    extra = extra + (ice_sum[0] + ice_sum[1]) + pltpu.roll(ice_sum[0] - ice_sum[1], 32, 1)
    a_ref[pl.ds(4, DEV, stride=RIN), :] = extra


def forward(u, q, ice, mat, ker, th, tl):
    hbm = pl.BlockSpec(memory_space=pltpu.MemorySpace.HBM)
    vmem = pl.BlockSpec(memory_space=pltpu.VMEM)
    far = [pltpu.with_memory_space_constraint(x, pltpu.MemorySpace.HBM) for x in (u, q, ice, mat, ker, th, tl)]
    return pl.pallas_call(
        forward_kernel,
        in_specs=[hbm] * 7,
        out_specs=vmem,
        out_shape=jax.ShapeDtypeStruct((DEV * RIN, 128), F32),
        scratch_shapes=[
            pltpu.VMEM((2, 2, 384, QUART), BF16),
            pltpu.VMEM((128 + NJ, NLON), F32),
            pltpu.VMEM((2, NJ, NK, NLON), F32),
            pltpu.VMEM((NJ, NLON), jnp.int32),
            pltpu.VMEM((NK, NJ), jnp.int32),
            pltpu.VMEM((4, NK, NR), F32),
            pltpu.VMEM((2, 2, DEV, QUART), BF16),
            pltpu.VMEM((2, 2, DEV, QUART), BF16),
            pltpu.SemaphoreType.DMA((13,)),
        ],
        compiler_params=pltpu.CompilerParams(vmem_limit_bytes=24 << 20),
        name="forward",
    )(*far)


def lane_tables():
    shape = (NI, 128)
    lane = lax.broadcasted_iota(jnp.int32, shape, 1)
    row = lax.broadcasted_iota(jnp.int32, shape, 0)
    return shape, lane, row


def take(x, index):
    return jnp.take_along_axis(x, index, axis=1)


def load_materials(b_ref, mu_ref, dec_ref, con_ref, s_ref, st_ref, dc_ref, g_ref, r_ref):
    shape, lane, row = lane_tables()
    r = lane & 3
    for b in range(NB):
        extra = b_ref[pl.ds(b * RIN + 4, NI, stride=NB * RIN), :]
        mat = take(extra, 64 + (lane & 63))

        def look(ref):
            out = jnp.full(shape, ref[0], F32)
            for m in range(1, 8):
                out = jnp.where(mat == float(m), ref[m], out)
            return out

        stiff = look(mu_ref)
        st_ref[b] = stiff
        dc_ref[b] = look(dec_ref)
        r_ref[b] = look(con_ref)
        g_ref[b] = (RELAX / DIAG) / stiff
        layer = (r + (4 * b + 1)).astype(F32) * (LOAD / NR)
        for kk in range(2):
            s_ref[kk, b] = take(extra, kk * 32 + (lane >> 2)) * layer


def three_sweeps(p, gain_ref, bufs, q_ref, q_out, s_ref, st_ref, dc_ref, g_ref):
    shape, lane, row = lane_tables()
    r = lane & 3
    j = (lane >> 2) & 15
    rp = (lane & ~3) | ((lane + 1) & 3)
    rm = (lane & ~3) | ((lane + 3) & 3)
    jp = (lane & 64) | ((lane + 4) & 63)
    jm = (lane & 64) | ((lane + 60) & 63)
    gains = [jnp.where(lane < 64, gain_ref[4 * p + 2 * kk], gain_ref[4 * p + 2 * kk + 1]) for kk in range(2)]
    zero = jnp.zeros(shape, F32)
    for buf in bufs[1:]:
        for kk in range(2):
            buf[kk, 0] = zero
            buf[kk, NB + 1] = zero
    for step in range(3):
        src, dst = bufs[step], bufs[step + 1]
        q_src = q_ref if step == 0 else q_out
        for kk in range(2):
            for b in range(NB):
                uc = src[kk, b + 1]
                up = src[kk, b + 2]
                dn = src[kk, b]
                ip = jnp.where(row == NI - 1, 0.0, pltpu.roll(uc, NI - 1, 0))
                im = jnp.where(row == 0, 0.0, pltpu.roll(uc, 1, 0))
                beside = take(jnp.where(r == 0, up, uc), rp) + take(jnp.where(r == 3, dn, uc), rm)
                beside = beside + take(jnp.where(j == 0, ip, uc), jp) + take(jnp.where(j == 15, im, uc), jm)
                q = q_src[kk, b]
                un = gains[kk] * uc + g_ref[b] * (s_ref[kk, b] - q) + (RELAX / DIAG) * beside
                dst[kk, b + 1] = un
                q_out[kk, b] = dc_ref[b] * q + st_ref[b] * (un - uc)


def half_kernel(b_ref, o_ref):
    for t in range(2):
        o_ref[pl.ds(t * DEV, DEV), :] = b_ref[pl.ds(5 + t, DEV, stride=RIN), :]


def first_kernel(
    dev_ref, gain_ref, mu_ref, dec_ref, con_ref, b_ref, ph_ref, pl_ref, wt_ref,
    u3_ref, q_ref, s_ref, st_ref, dc_ref, g_ref, c_ref,
    ua_ref, ub_ref, r_ref, z_ref, rt_ref,
):
    p = dev_ref[0]
    par = p % 2
    load_materials(b_ref, mu_ref, dec_ref, con_ref, s_ref, st_ref, dc_ref, g_ref, r_ref)
    for kk in range(2):
        ua_ref[kk, 0] = jnp.zeros((NI, 128), F32)
        ua_ref[kk, NB + 1] = jnp.zeros((NI, 128), F32)
        for b in range(NB):
            ua_ref[kk, b + 1] = b_ref[pl.ds(b * RIN + kk, NI, stride=NB * RIN), :]
            q_ref[kk, b] = b_ref[pl.ds(b * RIN + 2 + kk, NI, stride=NB * RIN), :]
    bufs = (ua_ref, ub_ref, ua_ref, u3_ref)
    three_sweeps(p, gain_ref, bufs, q_ref, q_ref, s_ref, st_ref, dc_ref, g_ref)
    for h in range(NB // 2):
        pair = [r_ref[2 * h + t] * u3_ref[0, 2 * h + t + 1] for t in range(2)]
        rt_ref[:, 128 * h : 128 * h + 128] = jnp.concatenate(pair, axis=0).T
    kept = rt_ref[pl.ds(pl.multiple_of(64 * par, 64), 64), :]
    for jj in range(NJ):
        for b in range(NB):
            z_ref[4 * b : 4 * b + 4, 64 * jj : 64 * jj + 64] = kept[4 * jj : 4 * jj + 4, 64 * b : 64 * b + 64]
    z = z_ref[...]
    mean = jnp.sum(z) * (1.0 / (NLAT * NR))
    z = z - jnp.where(p == 0, mean, 0.0)
    z = z * wt_ref[...]
    z4 = jnp.concatenate([z, z, z, z], axis=0)
    zh, zl = split(z4)
    ph, plo = ph_ref[...], pl_ref[...]
    c_ref[...] = dot_nt(ph, zh) + (dot_nt(ph, zl) + dot_nt(plo, zh))


def second_kernel(
    dev_ref, gain_ref, b_ref, ph_ref, pl_ref, u3_ref, q3_ref, s3_ref, st_ref, dc_ref, g_ref, c_ref, k_ref, o_ref,
    ua_ref, ub_ref, q_ref, s_ref, rt_ref, phi_ref,
):
    p = dev_ref[0]
    par = p % 2
    core = (p // NB) % 2
    mine = pl.multiple_of(128 * core, 128)
    other = pl.multiple_of(128 - 128 * core, 128)
    lane1 = lax.broadcasted_iota(jnp.int32, (128, 128), 1)
    sub1 = lax.broadcasted_iota(jnp.int32, (128, 128), 0)
    phi = jnp.zeros((NDEG, 128), F32)
    coef_mine = c_ref[pl.ds(mine, 128), :]
    coef_other = c_ref[pl.ds(other, 128), :]
    for b in range(NB):
        prod = jnp.concatenate(
            [
                b_ref[pl.ds(b * RIN + 5 + t, NI, stride=NB * RIN), :] * coef_mine[64 * t : 64 * t + 64]
                for t in range(2)
            ]
            + [
                k_ref[pl.ds(t * DEV + b, NI, stride=NB), :] * coef_other[64 * t : 64 * t + 64]
                for t in range(2)
            ],
            axis=0,
        )
        pick = (lane1 == (sub1 >> 5) + 4 * b).astype(BF16)
        hi, lo = split(prod)
        phi = phi + (dot_nn(hi, pick) + dot_nn(lo, pick))
    factor = jnp.where(p == 0, 2.0, jnp.where(p == MODES, 0.0, 1.0))
    phi_ref[pl.ds(mine, 128), :] = phi[:128] * factor
    phi_ref[pl.ds(other, 128), :] = phi[128:] * factor
    fh, fl = split(phi_ref[...].T[0:NR])
    ph, plo = ph_ref[...], pl_ref[...]
    pot = dot_nn(fh, ph) + (dot_nn(fl, ph) + dot_nn(fh, plo))
    rt_ref[...] = jnp.zeros(rt_ref.shape, F32)
    kept_ref = rt_ref.at[pl.ds(pl.multiple_of(64 * par, 64), 64), :]
    for jj in range(NJ):
        for b in range(NB):
            kept_ref[4 * jj : 4 * jj + 4, 64 * b : 64 * b + 64] = pot[4 * b : 4 * b + 4, 64 * jj : 64 * jj + 64]
    for h in range(NB // 2):
        back = rt_ref[:, 128 * h : 128 * h + 128].T
        for t in range(2):
            b = 2 * h + t
            piece = back[64 * t : 64 * t + 64]
            o_ref[pl.ds(b * ROUT + 4, NI, stride=NB * ROUT), :] = piece
            s_ref[0, b] = s3_ref[0, b] + COUPLE * piece
            s_ref[1, b] = s3_ref[1, b]
    bufs = (u3_ref, ua_ref, ub_ref, ua_ref)
    three_sweeps(p, gain_ref, bufs, q3_ref, q_ref, s_ref, st_ref, dc_ref, g_ref)
    for b in range(NB):
        for kk in range(2):
            o_ref[pl.ds(b * ROUT + kk, NI, stride=NB * ROUT), :] = ua_ref[kk, b + 1]
            o_ref[pl.ds(b * ROUT + 2 + kk, NI, stride=NB * ROUT), :] = q_ref[kk, b]


FIELD = (NB, NI, 128)


def local_call(kernel, name, scalars, arrays, out_shape, scratch):
    smem = pl.BlockSpec(memory_space=pltpu.SMEM)
    vmem = pl.BlockSpec(memory_space=pltpu.VMEM)
    return pl.pallas_call(
        kernel,
        in_specs=[smem] * len(scalars) + [vmem] * len(arrays),
        out_specs=jax.tree.map(lambda _: vmem, out_shape),
        out_shape=out_shape,
        scratch_shapes=[pltpu.VMEM(shape, F32) for shape in scratch],
        compiler_params=pltpu.CompilerParams(vmem_limit_bytes=16 << 20),
        name=name,
    )(*scalars, *arrays)


def inverse_kernel(b_ref, th_ref, tl_ref, u_hbm, q_hbm, p_hbm, y_ref, out_ref, sem):
    for f in range(3):
        slot = [b_ref[pl.ds(4 if f == 2 else 2 * f + kk, DEV, stride=ROUT), :] for kk in range(1 if f == 2 else 2)]
        pair = [slot[0].T] * 2 if f == 2 else [(slot[0] + slot[1]).T, (slot[0] - slot[1]).T]
        for e in range(2):
            hi, lo = split(pair[e])
            for k2 in range(2):
                y_ref[k2, e, 64 * f : 64 * f + 64, :] = hi[64 * k2 : 64 * k2 + 64]
                y_ref[k2, e, 192 + 64 * f : 256 + 64 * f, :] = lo[64 * k2 : 64 * k2 + 64]
    parity = lax.broadcasted_iota(jnp.int32, (192, 128), 1) & 1
    copies = []
    for n in range(2):
        cols = slice(256 * n, 256 * n + 256)
        halves = []
        for k2 in range(2):
            made = []
            for e in range(2):
                y = y_ref[k2, e]
                th, tl = th_ref[k2, e, :, cols], tl_ref[k2, e, :, cols]
                r1 = dot_nn(y, th)
                made.append(r1[:192] + (r1[192:] + dot_nn(y[:192], tl)))
            halves.append(made)
        for t in range(2):
            m = 2 * n + t
            both = []
            for k2 in range(2):
                even, odd = (x[:, 128 * t : 128 * t + 128] for x in halves[k2])
                both.append(
                    (
                        jnp.where(parity == 0, even, pltpu.roll(odd, 1, 1)),
                        jnp.where(parity == 0, pltpu.roll(even, 127, 1), odd),
                    )
                )
            for v in range(2):
                for base, value in ((0, both[0][v] + both[1][v]), (HALF, both[0][v] - both[1][v])):
                    start = base + 256 * m + 128 * v
                    for f in range(3):
                        for j in range(NJ):
                            row = 64 * f + 4 * j
                            out_ref[f, j, :, start : start + 128] = value[row : row + 4]
        for f, ref in enumerate((u_hbm, q_hbm, p_hbm)):
            for h in range(2):
                span = pl.ds(HALF * h + 512 * n, 512)
                copy = pltpu.make_async_copy(out_ref.at[f, :, :, span], ref.at[:, :, span], sem.at[n, f, h])
                copy.start()
                copies.append(copy)
    for copy in copies:
        copy.wait()


def inverse(b, th, tl):
    hbm = pl.BlockSpec(memory_space=pltpu.MemorySpace.HBM)
    vmem = pl.BlockSpec(memory_space=pltpu.VMEM)
    shape = (NJ, NK, NLON)
    return pl.pallas_call(
        inverse_kernel,
        in_specs=[vmem] * 3,
        out_specs=[hbm] * 3,
        out_shape=[jax.ShapeDtypeStruct(shape, F32)] * 3,
        scratch_shapes=[
            pltpu.VMEM((2, 2, 384, DEV), BF16),
            pltpu.VMEM((3, *shape), F32),
            pltpu.SemaphoreType.DMA((2, 3, 2)),
        ],
        compiler_params=pltpu.CompilerParams(vmem_limit_bytes=16 << 20),
        name="inverse",
    )(b, th, tl)


def exchange(x, rows):
    x = x.reshape(DEV, rows * 128)
    x = lax.all_to_all(x, ALL, split_axis=0, concat_axis=0, tiled=True)
    return x.reshape(DEV * rows, 128)


def solution(mesh):
    torus = Mesh(mesh.devices.reshape(4, 8, 2, 4, 2), ALL)
    th_np, tl_np, gain_np = fourier_tables()
    ph_np, pl_np, wt_np = legendre_tables()

    def per_device(
        displacement, memory, ice_class, material, mu_table, decay_table, contrast_table, gravity_kernel
    ):
        th, tl = jnp.asarray(th_np), jnp.asarray(tl_np)
        dev = lax.axis_index(ALL).reshape(1)
        packed = forward(displacement, memory, ice_class, material.T, gravity_kernel, th, tl)
        arrived = exchange(packed, RIN)
        half = local_call(half_kernel, "half", (), (arrived,), jax.ShapeDtypeStruct((DEV * 2, 128), F32), [])
        swapped = lax.ppermute(half, "lat_2", [(0, 1), (1, 0)])
        scalars = (dev, jnp.asarray(gain_np), mu_table, decay_table, contrast_table)
        ph, plo = jnp.asarray(ph_np), jnp.asarray(pl_np)
        padded, field = (2, NB + 2, NI, 128), (2, *FIELD)
        shapes = (padded, field, field, FIELD, FIELD, FIELD, (NDEG, 128))
        state = local_call(
            first_kernel, "first", scalars, (arrived, ph, plo, jnp.asarray(wt_np)),
            [jax.ShapeDtypeStruct(shape, F32) for shape in shapes],
            [padded, padded, FIELD, (NR, NLAT), (128, DEV)],
        )
        moved = local_call(
            second_kernel, "second", scalars[:2], (arrived, ph, plo, *state, swapped),
            jax.ShapeDtypeStruct((DEV * ROUT, 128), F32),
            [padded, padded, field, field, (128, DEV), (NDEG, 128)],
        )
        returned = exchange(moved, ROUT)
        return tuple(inverse(returned, th, tl))

    in_specs = (
        P(LAT, RAD, None),
        P(LAT, RAD, None),
        P(LAT, None),
        P(LAT, RAD),
        P(),
        P(),
        P(),
        P(LAT, RAD, None),
    )
    out_specs = (P(LAT, RAD, None), P(LAT, RAD, None), P(LAT, RAD, None))
    return jax.shard_map(per_device, mesh=torus, in_specs=in_specs, out_specs=out_specs, check_vma=False)
```

```python
import numpy as np
import jax
import jax.numpy as jnp
import ml_dtypes
from jax import lax
from jax.experimental import pallas as pl
from jax.experimental.pallas import tpu as pltpu
from jax.sharding import Mesh
from jax.sharding import PartitionSpec as P

LAT = ("lat_0", "lat_1", "lat_2")
RAD = ("rad_0", "rad_1")
ALL = LAT + RAD

NLON, NLAT, NR, MODES, NDEG = 2048, 1024, 32, 256, 256
DEV, NI, NB, NJ, NK = 512, 64, 8, 16, 4
HALF = NLON // 2
RIN, ROUT = 7, 5
LOAD, SHIFT, RELAX, COUPLE = 0.5, 0.5, 0.8, 2.0
DIAG = 6.0 + SHIFT
F32, BF16 = jnp.float32, jnp.bfloat16


def split_np(x):
    hi = x.astype(np.float32).astype(ml_dtypes.bfloat16)
    lo = (x - hi.astype(np.float64)).astype(np.float32).astype(ml_dtypes.bfloat16)
    return hi, lo


def fourier_tables():
    kind = np.zeros((2, DEV), np.int64)
    order = np.zeros((2, DEV), np.int64)
    for par in range(2):
        rest = iter([(k, c) for c in range(MODES + par, 2 * MODES, 2) for k in (0, 1)])
        for p in range(DEV):
            if p % 2 == par:
                k, c = (0, p) if p < MODES else (1, p - MODES)
            else:
                k, c = next(rest)
            kind[par, p], order[par, p] = k, c
    order[0, MODES] = HALF // 2
    l = np.arange(HALF)
    angle = (order[..., None] * l) % NLON * (2.0 * np.pi / NLON)
    cos, sin = np.cos(angle), np.sin(angle)
    value = np.where(kind[..., None] == 0, cos, sin) * np.sqrt(2.0 / NLON)
    value[0, 0] = np.sqrt(1.0 / NLON)
    value[0, MODES] = (cos[0, MODES] + sin[0, MODES]) * np.sqrt(1.0 / NLON)
    block, t = np.arange(HALF // 2) // 128, np.arange(HALF // 2) % 128
    even = 256 * block + np.where(t % 2 == 0, t, 128 + t - 1)
    odd = 256 * block + np.where(t % 2 == 0, t + 1, 128 + t)
    value = np.stack([value[..., even], value[..., odd]], axis=1)
    eigen = 2.0 * np.cos(order * (2.0 * np.pi / NLON))
    eigen = np.stack([eigen, -eigen])
    gain = (1.0 - RELAX) + RELAX / DIAG * eigen
    hi, lo = split_np(value)
    return hi, lo, np.ascontiguousarray(gain.transpose(2, 0, 1).reshape(DEV * 4)).astype(np.float32)


def legendre_tables():
    theta = (np.arange(NLAT) + 0.5) * (np.pi / NLAT)
    mu = np.cos(theta)
    rows = np.zeros((NDEG, NLAT))
    before, current = np.zeros(NLAT), np.ones(NLAT)
    for n in range(NDEG):
        rows[n] = current * np.sqrt(n + 0.5)
        before, current = current, ((2 * n + 1) * mu * current - n * before) / (n + 1)
    weight = np.pi / NLAT * np.sin(theta)
    rows = rows.reshape(NI, 4, NLAT).transpose(1, 0, 2).reshape(NDEG, NI, NJ)
    rows = rows.transpose(0, 2, 1).reshape(NDEG, NLAT)
    weight = weight.reshape(NI, NJ).T.reshape(1, NLAT)
    hi, lo = split_np(rows)
    return hi, lo, weight.astype(np.float32)


def split(x):
    hi = x.astype(BF16)
    return hi, (x - hi.astype(F32)).astype(BF16)


def dot_nt(a, b):
    return lax.dot_general(a, b, (((1,), (1,)), ((), ())), preferred_element_type=F32)


def dot_nn(a, b):
    return lax.dot_general(a, b, (((1,), (0,)), ((), ())), preferred_element_type=F32)


QUART = HALF // 2


def forward_kernel(
    u_hbm, q_hbm, ice_hbm, mat_hbm, ker_hbm, th_hbm, tl_hbm, a_ref,
    x_ref, w_ref, f_ref, ice_ref, mat_ref, ker_ref, th_ref, tl_ref, sem,
):
    copies = [
        pltpu.make_async_copy(u_hbm, f_ref.at[0], sem.at[0]),
        pltpu.make_async_copy(q_hbm, f_ref.at[1], sem.at[1]),
        pltpu.make_async_copy(ice_hbm, ice_ref, sem.at[2]),
        pltpu.make_async_copy(mat_hbm, mat_ref, sem.at[3]),
        pltpu.make_async_copy(ker_hbm, ker_ref, sem.at[4]),
    ]
    for k2 in range(2):
        for e in range(2):
            n = 5 + 4 * k2 + 2 * e
            copies.append(pltpu.make_async_copy(th_hbm.at[k2, e], th_ref.at[k2, e], sem.at[n]))
            copies.append(pltpu.make_async_copy(tl_hbm.at[k2, e], tl_ref.at[k2, e], sem.at[n + 1]))
    for copy in copies:
        copy.start()
    peer = lax.broadcasted_iota(jnp.int32, (DEV, 128), 0)
    lane = lax.broadcasted_iota(jnp.int32, (DEV, 128), 1)
    core = (peer >> 3) & 1
    x_ref[:, :, 256:, :] = jnp.zeros((2, 2, 128, QUART), BF16)
    copies[3].wait()
    copies[4].wait()
    ker = jnp.concatenate([ker_ref[:, rr, :] for rr in range(NK)], axis=1)
    for t in range(2):
        a_ref[pl.ds(5 + t, DEV, stride=RIN), :] = jnp.where(core == 0, ker[t : t + 1], ker[2 + t : 3 + t])
    place = lax.broadcasted_iota(jnp.int32, (NJ, 128), 0)
    column = lax.broadcasted_iota(jnp.int32, (NJ, 128), 1)
    spread = ((column >> 2) == place + NJ).astype(BF16)
    mat = dot_nn(mat_ref[...].astype(F32).astype(BF16), spread)
    mat = jnp.where((lane[:NK] & 3) == peer[:NK], mat, 0.0)
    extra = jnp.broadcast_to(jnp.sum(mat, axis=0, keepdims=True), (DEV, 128))
    for f in range(2):
        copies[f].wait()
        for j in range(NJ):
            w_ref[pl.ds(64 * f + 4 * j, 4), :] = f_ref[f, j]
    copies[2].wait()
    w_ref[pl.ds(128, NJ), :] = ice_ref[...].astype(F32)
    rows = 128 + NJ
    parity = lax.broadcasted_iota(jnp.int32, (rows, 128), 1) & 1
    def build(k2):
        for m in range(HALF // 256):
            v = []
            for t in range(2):
                start = 256 * m + 128 * t
                low, high = w_ref[:, start : start + 128], w_ref[:, HALF + start : HALF + start + 128]
                v.append(low + high if k2 == 0 else low - high)
            for e, value in (
                (0, jnp.where(parity == 0, v[0], pltpu.roll(v[1], 1, 1))),
                (1, jnp.where(parity == 0, pltpu.roll(v[0], 127, 1), v[1])),
            ):
                hi, lo = split(value[:128])
                cols = slice(128 * m, 128 * m + 128)
                x_ref[k2, e, 0:128, cols] = lo
                x_ref[k2, e, 128:256, cols] = hi
                x_ref[k2, e, 256 + NJ * k2 : 256 + NJ * k2 + NJ, cols] = value[128:].astype(BF16)

    first = lane < 64
    slots = []
    ice_sum = [0.0, 0.0]
    build(0)
    for k2 in range(2):
        for copy in copies[5 + 4 * k2 : 9 + 4 * k2]:
            copy.wait()
        product = []
        for e in range(2):
            x = x_ref[k2, e]
            r1 = dot_nt(th_ref[k2, e], x)
            r2 = dot_nt(tl_ref[k2, e], x[128:])
            product.append(r1[:, 128:256] + (r1[:, :128] + r2[:, :128]))
            ice_sum[e] = ice_sum[e] + (r1[:, 256:] + r2[:, 128:])
        if k2 == 0:
            build(1)
        slots.append((product[0] + product[1], product[0] - product[1]))
    for kk in range(2):
        even, odd = slots[0][kk], slots[1][kk]
        a_ref[pl.ds(kk, DEV, stride=RIN), :] = jnp.where(first, even, pltpu.roll(odd, 64, 1))
        a_ref[pl.ds(2 + kk, DEV, stride=RIN), :] = jnp.where(first, pltpu.roll(even, 64, 1), odd)
    extra = extra + (ice_sum[0] + ice_sum[1]) + pltpu.roll(ice_sum[0] - ice_sum[1], 32, 1)
    a_ref[pl.ds(4, DEV, stride=RIN), :] = extra


def forward(u, q, ice, mat, ker, th, tl):
    hbm = pl.BlockSpec(memory_space=pltpu.MemorySpace.HBM)
    vmem = pl.BlockSpec(memory_space=pltpu.VMEM)
    far = [pltpu.with_memory_space_constraint(x, pltpu.MemorySpace.HBM) for x in (u, q, ice, mat, ker, th, tl)]
    return pl.pallas_call(
        forward_kernel,
        in_specs=[hbm] * 7,
        out_specs=vmem,
        out_shape=jax.ShapeDtypeStruct((DEV * RIN, 128), F32),
        scratch_shapes=[
            pltpu.VMEM((2, 2, 384, QUART), BF16),
            pltpu.VMEM((128 + NJ, NLON), F32),
            pltpu.VMEM((2, NJ, NK, NLON), F32),
            pltpu.VMEM((NJ, NLON), jnp.int32),
            pltpu.VMEM((NK, NJ), jnp.int32),
            pltpu.VMEM((4, NK, NR), F32),
            pltpu.VMEM((2, 2, DEV, QUART), BF16),
            pltpu.VMEM((2, 2, DEV, QUART), BF16),
            pltpu.SemaphoreType.DMA((13,)),
        ],
        compiler_params=pltpu.CompilerParams(vmem_limit_bytes=24 << 20),
        name="forward",
    )(*far)


def lane_tables():
    shape = (NI, 128)
    lane = lax.broadcasted_iota(jnp.int32, shape, 1)
    row = lax.broadcasted_iota(jnp.int32, shape, 0)
    return shape, lane, row


def take(x, index):
    return jnp.take_along_axis(x, index, axis=1)


def load_materials(b_ref, mu_ref, dec_ref, con_ref, s_ref, st_ref, dc_ref, g_ref, r_ref):
    shape, lane, row = lane_tables()
    r = lane & 3
    for b in range(NB):
        extra = b_ref[pl.ds(b * RIN + 4, NI, stride=NB * RIN), :]
        mat = take(extra, 64 + (lane & 63))

        def look(ref):
            out = jnp.full(shape, ref[0], F32)
            for m in range(1, 8):
                out = jnp.where(mat == float(m), ref[m], out)
            return out

        stiff = look(mu_ref)
        st_ref[b] = stiff
        dc_ref[b] = look(dec_ref)
        r_ref[b] = look(con_ref)
        g_ref[b] = (RELAX / DIAG) / stiff
        layer = (r + (4 * b + 1)).astype(F32) * (LOAD / NR)
        for kk in range(2):
            s_ref[kk, b] = take(extra, kk * 32 + (lane >> 2)) * layer


def three_sweeps(p, gain_ref, bufs, q_ref, q_out, s_ref, st_ref, dc_ref, g_ref):
    shape, lane, row = lane_tables()
    r = lane & 3
    j = (lane >> 2) & 15
    rp = (lane & ~3) | ((lane + 1) & 3)
    rm = (lane & ~3) | ((lane + 3) & 3)
    jp = (lane & 64) | ((lane + 4) & 63)
    jm = (lane & 64) | ((lane + 60) & 63)
    gains = [jnp.where(lane < 64, gain_ref[4 * p + 2 * kk], gain_ref[4 * p + 2 * kk + 1]) for kk in range(2)]
    zero = jnp.zeros(shape, F32)
    for buf in bufs[1:]:
        for kk in range(2):
            buf[kk, 0] = zero
            buf[kk, NB + 1] = zero
    for step in range(3):
        src, dst = bufs[step], bufs[step + 1]
        q_src = q_ref if step == 0 else q_out
        for kk in range(2):
            for b in range(NB):
                uc = src[kk, b + 1]
                up = src[kk, b + 2]
                dn = src[kk, b]
                ip = jnp.where(row == NI - 1, 0.0, pltpu.roll(uc, NI - 1, 0))
                im = jnp.where(row == 0, 0.0, pltpu.roll(uc, 1, 0))
                beside = take(jnp.where(r == 0, up, uc), rp) + take(jnp.where(r == 3, dn, uc), rm)
                beside = beside + take(jnp.where(j == 0, ip, uc), jp) + take(jnp.where(j == 15, im, uc), jm)
                q = q_src[kk, b]
                un = gains[kk] * uc + g_ref[b] * (s_ref[kk, b] - q) + (RELAX / DIAG) * beside
                dst[kk, b + 1] = un
                q_out[kk, b] = dc_ref[b] * q + st_ref[b] * (un - uc)


def half_kernel(b_ref, o_ref):
    for t in range(2):
        o_ref[pl.ds(t * DEV, DEV), :] = b_ref[pl.ds(5 + t, DEV, stride=RIN), :]


def first_kernel(
    dev_ref, gain_ref, mu_ref, dec_ref, con_ref, b_ref, ph_ref, pl_ref, wt_ref,
    u3_ref, q_ref, s_ref, st_ref, dc_ref, g_ref, c_ref,
    ua_ref, ub_ref, r_ref, z_ref, rt_ref,
):
    p = dev_ref[0]
    par = p % 2
    load_materials(b_ref, mu_ref, dec_ref, con_ref, s_ref, st_ref, dc_ref, g_ref, r_ref)
    for kk in range(2):
        ua_ref[kk, 0] = jnp.zeros((NI, 128), F32)
        ua_ref[kk, NB + 1] = jnp.zeros((NI, 128), F32)
        for b in range(NB):
            ua_ref[kk, b + 1] = b_ref[pl.ds(b * RIN + kk, NI, stride=NB * RIN), :]
            q_ref[kk, b] = b_ref[pl.ds(b * RIN + 2 + kk, NI, stride=NB * RIN), :]
    bufs = (ua_ref, ub_ref, ua_ref, u3_ref)
    three_sweeps(p, gain_ref, bufs, q_ref, q_ref, s_ref, st_ref, dc_ref, g_ref)
    for h in range(NB // 2):
        pair = [r_ref[2 * h + t] * u3_ref[0, 2 * h + t + 1] for t in range(2)]
        rt_ref[:, 128 * h : 128 * h + 128] = jnp.concatenate(pair, axis=0).T
    kept = rt_ref[pl.ds(pl.multiple_of(64 * par, 64), 64), :]
    for jj in range(NJ):
        for b in range(NB):
            z_ref[4 * b : 4 * b + 4, 64 * jj : 64 * jj + 64] = kept[4 * jj : 4 * jj + 4, 64 * b : 64 * b + 64]
    z = z_ref[...]
    mean = jnp.sum(z) * (1.0 / (NLAT * NR))
    z = z - jnp.where(p == 0, mean, 0.0)
    z = z * wt_ref[...]
    z4 = jnp.concatenate([z, z, z, z], axis=0)
    zh, zl = split(z4)
    ph, plo = ph_ref[...], pl_ref[...]
    c_ref[...] = dot_nt(ph, zh) + (dot_nt(ph, zl) + dot_nt(plo, zh))


def second_kernel(
    dev_ref, gain_ref, b_ref, ph_ref, pl_ref, u3_ref, q3_ref, s3_ref, st_ref, dc_ref, g_ref, c_ref, k_ref, o_ref,
    ua_ref, ub_ref, q_ref, s_ref, rt_ref, phi_ref,
):
    p = dev_ref[0]
    par = p % 2
    core = (p // NB) % 2
    mine = pl.multiple_of(128 * core, 128)
    other = pl.multiple_of(128 - 128 * core, 128)
    coef_mine = c_ref[pl.ds(mine, 128), :]
    coef_other = c_ref[pl.ds(other, 128), :]
    products = []
    for b in range(NB):
        products.append(
            jnp.concatenate(
                [
                    b_ref[pl.ds(b * RIN + 5 + t, NI, stride=NB * RIN), :] * coef_mine[64 * t : 64 * t + 64]
                    for t in range(2)
                ]
                + [
                    k_ref[pl.ds(t * DEV + b, NI, stride=NB), :] * coef_other[64 * t : 64 * t + 64]
                    for t in range(2)
                ],
                axis=0,
            )
        )
    lane1 = lax.broadcasted_iota(jnp.int32, (128 * NB, 128), 1)
    sub1 = lax.broadcasted_iota(jnp.int32, (128 * NB, 128), 0)
    pick = (lane1 == (sub1 >> 5)).astype(BF16)
    hi, lo = split(jnp.concatenate(products, axis=1))
    phi = dot_nn(hi, pick) + dot_nn(lo, pick)
    factor = jnp.where(p == 0, 2.0, jnp.where(p == MODES, 0.0, 1.0))
    phi_ref[pl.ds(mine, 128), :] = phi[:128] * factor
    phi_ref[pl.ds(other, 128), :] = phi[128:] * factor
    fh, fl = split(phi_ref[...].T[0:NR])
    ph, plo = ph_ref[...], pl_ref[...]
    pot = dot_nn(fh, ph) + (dot_nn(fl, ph) + dot_nn(fh, plo))
    rt_ref[...] = jnp.zeros(rt_ref.shape, F32)
    kept_ref = rt_ref.at[pl.ds(pl.multiple_of(64 * par, 64), 64), :]
    for jj in range(NJ):
        for b in range(NB):
            kept_ref[4 * jj : 4 * jj + 4, 64 * b : 64 * b + 64] = pot[4 * b : 4 * b + 4, 64 * jj : 64 * jj + 64]
    for h in range(NB // 2):
        back = rt_ref[:, 128 * h : 128 * h + 128].T
        for t in range(2):
            b = 2 * h + t
            piece = back[64 * t : 64 * t + 64]
            o_ref[pl.ds(b * ROUT + 4, NI, stride=NB * ROUT), :] = piece
            s_ref[0, b] = s3_ref[0, b] + COUPLE * piece
            s_ref[1, b] = s3_ref[1, b]
    bufs = (u3_ref, ua_ref, ub_ref, ua_ref)
    three_sweeps(p, gain_ref, bufs, q3_ref, q_ref, s_ref, st_ref, dc_ref, g_ref)
    for b in range(NB):
        for kk in range(2):
            o_ref[pl.ds(b * ROUT + kk, NI, stride=NB * ROUT), :] = ua_ref[kk, b + 1]
            o_ref[pl.ds(b * ROUT + 2 + kk, NI, stride=NB * ROUT), :] = q_ref[kk, b]


FIELD = (NB, NI, 128)


def local_call(kernel, name, scalars, arrays, out_shape, scratch):
    smem = pl.BlockSpec(memory_space=pltpu.SMEM)
    vmem = pl.BlockSpec(memory_space=pltpu.VMEM)
    return pl.pallas_call(
        kernel,
        in_specs=[smem] * len(scalars) + [vmem] * len(arrays),
        out_specs=jax.tree.map(lambda _: vmem, out_shape),
        out_shape=out_shape,
        scratch_shapes=[pltpu.VMEM(shape, F32) for shape in scratch],
        compiler_params=pltpu.CompilerParams(vmem_limit_bytes=16 << 20),
        name=name,
    )(*scalars, *arrays)


def inverse_kernel(b_ref, th_ref, tl_ref, u_hbm, q_hbm, p_hbm, y_ref, out_ref, sem):
    for f in range(3):
        slot = [b_ref[pl.ds(4 if f == 2 else 2 * f + kk, DEV, stride=ROUT), :] for kk in range(1 if f == 2 else 2)]
        pair = [slot[0].T] * 2 if f == 2 else [(slot[0] + slot[1]).T, (slot[0] - slot[1]).T]
        for e in range(2):
            hi, lo = split(pair[e])
            for k2 in range(2):
                y_ref[k2, e, 64 * f : 64 * f + 64, :] = hi[64 * k2 : 64 * k2 + 64]
                y_ref[k2, e, 192 + 64 * f : 256 + 64 * f, :] = lo[64 * k2 : 64 * k2 + 64]
    parity = lax.broadcasted_iota(jnp.int32, (64, 128), 1) & 1
    copies = []
    for n in range(2):
        cols = slice(256 * n, 256 * n + 256)
        halves = []
        for k2 in range(2):
            made = []
            for e in range(2):
                y = y_ref[k2, e]
                th, tl = th_ref[k2, e, :, cols], tl_ref[k2, e, :, cols]
                r1 = dot_nn(y, th)
                made.append(r1[:192] + (r1[192:] + dot_nn(y[:192], tl)))
            halves.append(made)
        for f, ref in enumerate((u_hbm, q_hbm, p_hbm)):
            rows = slice(64 * f, 64 * f + 64)
            for t in range(2):
                both = []
                for k2 in range(2):
                    even, odd = (x[rows, 128 * t : 128 * t + 128] for x in halves[k2])
                    both.append(
                        (
                            jnp.where(parity == 0, even, pltpu.roll(odd, 1, 1)),
                            jnp.where(parity == 0, pltpu.roll(even, 127, 1), odd),
                        )
                    )
                for v in range(2):
                    start = 512 * n + 256 * t + 128 * v
                    for base, value in ((0, both[0][v] + both[1][v]), (HALF, both[0][v] - both[1][v])):
                        for j in range(NJ):
                            out_ref[f, j, :, base + start : base + start + 128] = value[4 * j : 4 * j + 4]
            for h in range(2):
                span = pl.ds(HALF * h + 512 * n, 512)
                copy = pltpu.make_async_copy(out_ref.at[f, :, :, span], ref.at[:, :, span], sem.at[n, f, h])
                copy.start()
                copies.append(copy)
    for copy in copies:
        copy.wait()


def inverse(b, th, tl):
    hbm = pl.BlockSpec(memory_space=pltpu.MemorySpace.HBM)
    vmem = pl.BlockSpec(memory_space=pltpu.VMEM)
    shape = (NJ, NK, NLON)
    return pl.pallas_call(
        inverse_kernel,
        in_specs=[vmem] * 3,
        out_specs=[hbm] * 3,
        out_shape=[jax.ShapeDtypeStruct(shape, F32)] * 3,
        scratch_shapes=[
            pltpu.VMEM((2, 2, 384, DEV), BF16),
            pltpu.VMEM((3, *shape), F32),
            pltpu.SemaphoreType.DMA((2, 3, 2)),
        ],
        compiler_params=pltpu.CompilerParams(vmem_limit_bytes=16 << 20),
        name="inverse",
    )(b, th, tl)


def exchange(x, rows):
    x = x.reshape(DEV, rows * 128)
    x = lax.all_to_all(x, ALL, split_axis=0, concat_axis=0, tiled=True)
    return x.reshape(DEV * rows, 128)


def solution(mesh):
    torus = Mesh(mesh.devices.reshape(4, 8, 2, 4, 2), ALL)
    th_np, tl_np, gain_np = fourier_tables()
    ph_np, pl_np, wt_np = legendre_tables()

    def per_device(
        displacement, memory, ice_class, material, mu_table, decay_table, contrast_table, gravity_kernel
    ):
        th, tl = jnp.asarray(th_np), jnp.asarray(tl_np)
        dev = lax.axis_index(ALL).reshape(1)
        packed = forward(displacement, memory, ice_class, material.T, gravity_kernel, th, tl)
        arrived = exchange(packed, RIN)
        half = local_call(half_kernel, "half", (), (arrived,), jax.ShapeDtypeStruct((DEV * 2, 128), F32), [])
        swapped = lax.ppermute(half, "lat_2", [(0, 1), (1, 0)])
        scalars = (dev, jnp.asarray(gain_np), mu_table, decay_table, contrast_table)
        ph, plo = jnp.asarray(ph_np), jnp.asarray(pl_np)
        padded, field = (2, NB + 2, NI, 128), (2, *FIELD)
        shapes = (padded, field, field, FIELD, FIELD, FIELD, (NDEG, 128))
        state = local_call(
            first_kernel, "first", scalars, (arrived, ph, plo, jnp.asarray(wt_np)),
            [jax.ShapeDtypeStruct(shape, F32) for shape in shapes],
            [padded, padded, FIELD, (NR, NLAT), (128, DEV)],
        )
        moved = local_call(
            second_kernel, "second", scalars[:2], (arrived, ph, plo, *state, swapped),
            jax.ShapeDtypeStruct((DEV * ROUT, 128), F32),
            [padded, padded, field, field, (128, DEV), (NDEG, 128)],
        )
        returned = exchange(moved, ROUT)
        return tuple(inverse(returned, th, tl))

    in_specs = (
        P(LAT, RAD, None),
        P(LAT, RAD, None),
        P(LAT, None),
        P(LAT, RAD),
        P(),
        P(),
        P(),
        P(LAT, RAD, None),
    )
    out_specs = (P(LAT, RAD, None), P(LAT, RAD, None), P(LAT, RAD, None))
    return jax.shard_map(per_device, mesh=torus, in_specs=in_specs, out_specs=out_specs, check_vma=False)
```
